512 devices in a mesh: gx: 32 (over x, y, core), gy: 16 (over z).
Axes of the slice: x: 4, y: 4, z: 16, core: 2. Of those that a mesh axis runs over, the one named last changes fastest.
Arguments:
- right_side: float32 [512, 256, 128], P('gx', 'gy'), may hold values from -24 to 24
- material: int32 [512, 256, 128], P('gx', 'gy'), may hold values from 0 to 15
- conductivity: float32 [16], replicated, may hold values from 0.2 to 5
Outputs:
- solution_field: float32 [512, 256, 128], P('gx', 'gy')
The draws below stay inside these ranges and needn't reach their ends.
All inputs are finite; a program needn't handle non-finite values.
Results may differ from the reference program's by a relative error of at most 0.0001.
Values sent between devices are 32-bit elements; how exact they have to be, the bound alone decides.
A program may use at most 64 MiB of HBM per device.

```python
import math
import jax
import jax.numpy as jnp

CYCLES = 2
COARSE_SWEEPS = 6
NMAT = 16
NX = 512
NY = 256
NZ = 128


def plant(drawn, key, smallest, largest):
    longest = drawn.shape.index(max(drawn.shape))
    spots = []
    for shift in (0, 1):
        where = [jax.random.randint(jax.random.fold_in(key, axis), (), 0, length) for axis, length in enumerate(drawn.shape)]
        where[longest] = (where[longest] + shift) % drawn.shape[longest]
        spots.append(tuple(where))
    return drawn.at[spots[0]].set(smallest).at[spots[1]].set(largest)


def block_levels(own_key, shape, pieces, least, high):
    def one(axis_at, blocks):
        heights = jax.random.uniform(jax.random.fold_in(jax.random.fold_in(own_key, 6), axis_at), (blocks,), jnp.float32, least / len(pieces), high / len(pieces))
        return jnp.repeat(jnp.exp(heights), shape[axis_at] // blocks).reshape((-1,) + (1,) * (len(shape) - axis_at - 1))

    level = one(*pieces[0])
    for cut in pieces[1:]:
        level = level * one(*cut)
    return level


def noise(own_key, extent, deviation, most, pieces=(), dtype=jnp.bfloat16):
    loudness = block_levels(own_key, extent, pieces, -0.22, 0.18) if pieces else 1.0
    values = jax.random.normal(own_key, extent, jnp.float32) * deviation * loudness
    return jnp.minimum(jnp.maximum(values, -most), most).astype(dtype)


def setup_inputs(seed: int = 0) -> dict:
    splits = jax.random.split(jax.random.key(seed), 4)
    return {
        "right_side": noise(splits[0], (NX, NY, NZ), 4.0, 24.0, ((0, 32), (1, 16)), jnp.float32),
        "material": plant(jax.random.randint(splits[1], (NX, NY, NZ), 0, NMAT), jax.random.fold_in(splits[1], 1), 0, NMAT - 1).astype(jnp.int32),
        "conductivity": jnp.clip(jnp.exp(jax.random.uniform(splits[2], (NMAT,), jnp.float32, math.log(0.2), math.log(5.0))), 0.2, 5.0),
    }


OMEGA = 0.8


def neighbours(padded):
    return (padded[2:, 1:-1, 1:-1], padded[:-2, 1:-1, 1:-1],
            padded[1:-1, 2:, 1:-1], padded[1:-1, :-2, 1:-1],
            padded[1:-1, 1:-1, 2:], padded[1:-1, 1:-1, :-2])


def face_set(padded_k, scale):
    centre = padded_k[1:-1, 1:-1, 1:-1]
    faces = tuple(0.5 * scale * (centre + other) for other in neighbours(padded_k))
    total = faces[0] + faces[1] + faces[2] + faces[3] + faces[4] + faces[5]
    return faces, total


def apply_operator(padded_field, faces, total):
    result = total * padded_field[1:-1, 1:-1, 1:-1]
    for weight, other in zip(faces, neighbours(padded_field)):
        result = result - weight * other
    return result


def restrict(field):
    sx, sy, sz = field.shape
    return field.reshape(sx // 2, 2, sy // 2, 2, sz // 2, 2).mean(axis=(1, 3, 5))


def prolong(field):
    return jnp.repeat(jnp.repeat(jnp.repeat(field, 2, 0), 2, 1), 2, 2)


def cycle(levels, level, field, right, first):
    faces, total = levels[level]
    if first:
        field = OMEGA * right / total
    else:
        field = field + OMEGA * (right - apply_operator(jnp.pad(field, 1), faces, total)) / total
    resid = right - apply_operator(jnp.pad(field, 1), faces, total)
    coarse_right = restrict(resid)
    if level == 2:
        cfaces, ctotal = levels[3]
        correction = OMEGA * coarse_right / ctotal
        for sweep in range(COARSE_SWEEPS - 1):
            correction = correction + OMEGA * (coarse_right - apply_operator(jnp.pad(correction, 1), cfaces, ctotal)) / ctotal
    else:
        correction = cycle(levels, level + 1, None, coarse_right, True)
    field = field + prolong(correction)
    field = field + OMEGA * (right - apply_operator(jnp.pad(field, 1), faces, total)) / total
    return field


def reference(right_side, material, conductivity):
    cond = conductivity[material]
    conds = [cond]
    for level in range(3):
        conds.append(restrict(conds[-1]))
    levels = [face_set(jnp.pad(conds[level], 1), 0.25 ** level) for level in range(4)]
    field = jnp.zeros_like(right_side)
    for turn in range(CYCLES):
        field = cycle(levels, 0, field, right_side, turn == 0)
    return field
```

```python
import functools

import jax
import jax.numpy as jnp
from jax import lax
from jax.experimental import pallas as pl
from jax.experimental.pallas import tpu as pltpu
from jax.sharding import PartitionSpec as P

MESH = pl.DeviceIdType.MESH
CYCLES = 2
SWEEPS = 6
OMEGA = 0.8
NMAT = 16
H = 8
R = 3
DIRS = tuple((a, b) for a in (-1, 0, 1) for b in (-1, 0, 1) if (a, b) != (0, 0))
OPP = tuple(DIRS.index((-a, -b)) for a, b in DIRS)
STEPS = tuple(d for d in range(-R, R + 1) if d)


def send_part(s):
    return {1: slice(8, 16), -1: slice(0, 8), 0: slice(0, 16)}[s]


def halo_part(s):
    return {1: slice(24, 32), -1: slice(0, 8), 0: slice(8, 24)}[s]


def roll(v, shift, axis):
    return pltpu.roll(v, shift % v.shape[axis], axis)


def iota(shape, axis):
    return lax.broadcasted_iota(jnp.int32, shape, axis)


def pair_swap(v, apart, axis):
    low = (iota(v.shape, axis) & apart) == 0
    return jnp.where(low, roll(v, -apart, axis), roll(v, apart, axis))


def kernel(nx, ny, cond, g_hbm, m_hbm, out, *refs):
    names = (
        "G", "M", "K0", "V", "VB", "VE", "I0", "T0", "X0", "YP0", "YM0", "ZP0", "ZM0", "S0", "S1",
        "F0", "K1", "V1", "G1", "VE1", "I1", "X1", "YP1", "YM1", "ZP1", "ZM1", "S2", "F1", "K2",
        "V2", "G2", "VF2", "VE2", "I2", "X2", "YP2", "YM2", "ZP2", "ZM2", "K3", "SX", "SY", "SC",
        "A", "B", "W", "lsem", "gs", "gr", "ms", "mr", "vs", "vr", "ss", "sr", "as_", "ar", "bs",
        "br",
    )
    r = dict(zip(names, refs, strict=True))
    px, py = lax.axis_index("gx"), lax.axis_index("gy")

    def exists(a, b=0):
        x, y = px + a, py + b
        return (x >= 0) & (x < nx) & (y >= 0) & (y < ny)

    def dev(a, b):
        return (px + a, py + b)

    own = (slice(8, 24), slice(8, 24))
    lg = pltpu.make_async_copy(g_hbm, r["G"].at[own], r["lsem"].at[0])
    lm = pltpu.make_async_copy(m_hbm, r["M"].at[own], r["lsem"].at[1])
    lg.start()
    lm.start()
    others = [(a, b) for a, b in DIRS] + [(d, 0) for d in STEPS if abs(d) > 1]
    others += [(0, d) for d in STEPS if abs(d) > 1]
    barrier = pltpu.get_barrier_semaphore()
    zero8 = jnp.zeros((8, 32, 128), jnp.float32)
    for name, fill in (("G", 0.0), ("VB", 0.0), ("M", NMAT)):
        ref = r[name]
        dt = ref.dtype
        for s in (slice(0, 8), slice(24, 32)):
            ref[s] = jnp.full((8, 32, 128), fill, dt)
            ref[8:24, s] = jnp.full((16, 8, 128), fill, dt)
    r["A"][...] = jnp.zeros(r["A"].shape, jnp.float32)
    r["B"][...] = jnp.zeros(r["B"].shape, jnp.float32)
    for n in ("SX", "SY", "SC"):
        r[n][...] = jnp.zeros(r[n].shape, jnp.float32)
    count = jnp.int32(0)
    for a, b in others:
        ok = exists(a, b)
        count = count + jnp.where(ok, 1, 0)

        @pl.when(ok)
        def _(a=a, b=b):
            pl.semaphore_signal(barrier, inc=1, device_id=dev(a, b), device_id_type=MESH)

    pl.semaphore_wait(barrier, count)

    def halo_copy(src, dst, ssem, rsem, i, sending):
        a, b = DIRS[i]
        if sending:
            there = (halo_part(-a), halo_part(-b))
            return pltpu.make_async_remote_copy(
                src_ref=src.at[send_part(a), send_part(b)],
                dst_ref=dst.at[there],
                send_sem=ssem.at[i],
                recv_sem=rsem.at[OPP[i]],
                device_id=dev(a, b),
                device_id_type=MESH,
            )
        here = dst.at[halo_part(a), halo_part(b)]
        return pltpu.make_async_remote_copy(
            src_ref=here, dst_ref=here, send_sem=ssem.at[i], recv_sem=rsem.at[i],
            device_id=dev(a, b), device_id_type=MESH,
        )

    def each(fn, dirs=range(len(DIRS))):
        for i in dirs:
            pl.when(exists(*DIRS[i]))(functools.partial(fn, i))

    def send_halo(src, dst, ssem, rsem):
        each(lambda i: halo_copy(src, dst, ssem, rsem, i, True).start())

    def recv_halo(dst, ssem, rsem):
        each(lambda i: halo_copy(None, dst, ssem, rsem, i, False).wait_recv())

    def sent_halo(src, dst, ssem, rsem):
        each(lambda i: halo_copy(src, dst, ssem, rsem, i, True).wait_send())

    send_halo(m_hbm, r["M"], r["ms"], r["mr"])
    send_halo(g_hbm, r["G"], r["gs"], r["gr"])

    lane = iota((8, 128), 1)
    table = jnp.zeros((8, 128), jnp.float32)
    for i in range(NMAT):
        table = jnp.where(lane == i, cond[i], table)
    lm.wait()
    recv_halo(r["M"], r["ms"], r["mr"])
    table32 = jnp.concatenate([table] * 4, 0)

    def look(i, _):
        r["K0"][i] = jnp.take_along_axis(table32, r["M"][i], axis=1)
        return 0

    lax.fori_loop(0, 32, look, 0)

    def faces(lv, planes, first, last):
        scale = 0.5 * 0.25**lv
        step = 1 << lv
        k_ref = r[f"K{lv}"]
        x_ref = r[f"X{lv}"]
        x_ref[first - 1] = scale * (k_ref[first - 1] + k_ref[first])

        def body(i, _):
            k = k_ref[i]
            ln = iota(k.shape, 1)
            wx = scale * (k + k_ref[i + 1])
            wm = x_ref[i - 1]
            yp = scale * (k + roll(k, -1, 0))
            ym = scale * (k + roll(k, 1, 0))
            zp = scale * (k + jnp.where(ln < 128 - step, roll(k, -step, 1), 0.0))
            zm = scale * (k + jnp.where(ln >= step, roll(k, step, 1), 0.0))
            total = wx + wm + yp + ym + zp + zm
            inside = k > 0.0
            x_ref[i] = wx
            r[f"YP{lv}"][i] = yp
            r[f"YM{lv}"][i] = ym
            r[f"ZP{lv}"][i] = jnp.where(ln < 128 - step, zp, 0.0)
            r[f"ZM{lv}"][i] = jnp.where(ln >= step, zm, 0.0)
            inv = jnp.where(inside, OMEGA / jnp.where(inside, total, 1.0), 0.0)
            r[f"I{lv}"][i] = inv
            if lv == 0:
                r["T0"][i] = total
                r["V"][i] = inv * r["G"][i]
            return 0

        lax.fori_loop(first, last, body, 0)

    def around(lv, v_ref, i):
        step = 1 << lv
        v = v_ref[i]
        x = r[f"X{lv}"]
        n = x[i] * v_ref[i + 1] + x[i - 1] * v_ref[i - 1]
        n = n + r[f"YP{lv}"][i] * roll(v, -1, 0) + r[f"YM{lv}"][i] * roll(v, 1, 0)
        return v, n + r[f"ZP{lv}"][i] * roll(v, -step, 1) + r[f"ZM{lv}"][i] * roll(v, step, 1)

    def z_mean(s, lv):
        return 0.125 * (s + pair_swap(s, 1 << lv, 1))

    def k1_sum(i, _):
        r["S0"][i] = r["K0"][2 * i] + r["K0"][2 * i + 1]
        return 0

    lax.fori_loop(0, 16, k1_sum, 0)

    def k1_mean(i, _):
        s = r["S0"][i, pl.ds(0, 16, 2), :] + r["S0"][i, pl.ds(1, 16, 2), :]
        r["K1"][i] = z_mean(s, 0)
        return 0

    lax.fori_loop(0, 16, k1_mean, 0)

    def k2_sum(i, _):
        r["S1"][i] = r["K1"][2 * i] + r["K1"][2 * i + 1]
        return 0

    lax.fori_loop(0, 8, k2_sum, 0)

    def k2_mean(i, _):
        s = r["S1"][i, pl.ds(0, 8, 2), :] + r["S1"][i, pl.ds(1, 8, 2), :]
        r["K2"][i] = z_mean(s, 1)
        return 0

    lax.fori_loop(0, 8, k2_mean, 0)

    def to_three(t):
        t = t + pair_swap(t, 1, 0)
        return z_mean(t, 2)

    for i in range(4):
        r["K3"][i] = to_three(r["K2"][2 * i] + r["K2"][2 * i + 1])

    scale3 = 0.5 * 0.25**3
    inv3 = []
    for i in (1, 2):
        k = r["K3"][i]
        s = r["K3"][i - 1] + r["K3"][i + 1] + roll(k, 2, 0) + roll(k, -2, 0)
        s = s + jnp.where(lane < 120, roll(k, -8, 1), 0.0) + jnp.where(lane >= 8, roll(k, 8, 1), 0.0)
        t = scale3 * (6.0 * k + s)
        ok = k > 0.0
        inv3.append(jnp.where(ok, OMEGA / jnp.where(ok, t, 1.0), 0.0))

    lg.wait()
    recv_halo(r["G"], r["gs"], r["gr"])
    faces(0, 32, 1, 31)
    faces(1, 16, 1, 15)
    faces(2, 8, 1, 7)

    row = iota((8, 128), 0)
    slot = lane & 7
    coarse_w = None

    def z_copies(d, cyc, sending):
        a = r["A"].at[cyc]
        if sending:
            return pltpu.make_async_remote_copy(
                src_ref=a.at[R], dst_ref=a.at[R - d], send_sem=r["as_"].at[cyc, d + R],
                recv_sem=r["ar"].at[cyc, R - d], device_id=dev(0, d), device_id_type=MESH,
            )
        return pltpu.make_async_remote_copy(
            src_ref=a.at[R + d], dst_ref=a.at[R + d], send_sem=r["as_"].at[cyc, d + R],
            recv_sem=r["ar"].at[cyc, R + d], device_id=dev(0, d), device_id_type=MESH,
        )

    def x_copies(d, cyc, sending):
        b = r["B"].at[cyc]

        def part(s):
            return b.at[pl.ds(8 * s, 8)]

        if sending:
            return pltpu.make_async_remote_copy(
                src_ref=part(R), dst_ref=part(R - d), send_sem=r["bs"].at[cyc, d + R],
                recv_sem=r["br"].at[cyc, R - d], device_id=dev(d, 0), device_id_type=MESH,
            )
        return pltpu.make_async_remote_copy(
            src_ref=part(R + d), dst_ref=part(R + d), send_sem=r["bs"].at[cyc, d + R],
            recv_sem=r["br"].at[cyc, R + d], device_id=dev(d, 0), device_id_type=MESH,
        )

    far_first = sorted(STEPS, key=lambda d: -abs(d))

    def side_buf(a, b, cyc):
        if b == 0:
            return r["SX"].at[cyc, (a + 1) // 2]
        if a == 0:
            return r["SY"].at[cyc, (b + 1) // 2]
        return r["SC"].at[cyc, (a + 1) + (b + 1) // 2]

    def side_src(a):
        return {1: slice(4, 6), -1: slice(2, 4), 0: slice(2, 6)}[a]

    def side_copy(i, cyc, sending):
        a, b = DIRS[i]
        if sending:
            return pltpu.make_async_remote_copy(
                src_ref=r["V2"].at[cyc, side_src(a)], dst_ref=side_buf(-a, -b, cyc),
                send_sem=r["ss"].at[cyc, i], recv_sem=r["sr"].at[cyc, OPP[i]],
                device_id=dev(a, b), device_id_type=MESH,
            )
        here = side_buf(a, b, cyc)
        return pltpu.make_async_remote_copy(
            src_ref=here, dst_ref=here, send_sem=r["ss"].at[cyc, i], recv_sem=r["sr"].at[cyc, i],
            device_id=dev(a, b), device_id_type=MESH,
        )

    for cyc in range(CYCLES):
        if cyc:
            recv_halo(r["VB"], r["vs"], r["vr"])

            def sweep(i, _):
                v, n = around(0, r["VB"], i)
                r["V"][i] = (1.0 - OMEGA) * v + r["I0"][i] * (r["G"][i] + n)
                return 0

            lax.fori_loop(1, 31, sweep, 0)

        def resid0(i, first=cyc == 0):
            v, n = around(0, r["V"], i)
            if first:
                return (1.0 - OMEGA) * r["G"][i] + n
            return r["G"][i] - r["T0"][i] * v + n

        def down0(i, _):
            r["S0"][i] = resid0(2 * i) + resid0(2 * i + 1)
            return 0

        lax.fori_loop(1, 15, down0, 0)

        def start1(i, _):
            s = r["S0"][i, pl.ds(0, 16, 2), :] + r["S0"][i, pl.ds(1, 16, 2), :]
            g = z_mean(s, 0)
            r["G1"][i] = g
            r["V1"][i] = r["I1"][i] * g
            return 0

        lax.fori_loop(1, 15, start1, 0)

        def resid1(i):
            _, n = around(1, r["V1"], i)
            return (1.0 - OMEGA) * r["G1"][i] + n

        def down1(i, _):
            r["S1"][i] = resid1(2 * i) + resid1(2 * i + 1)
            return 0

        lax.fori_loop(1, 7, down1, 0)
        v2 = r["V2"].at[cyc]

        def start2(i, _):
            s = r["S1"][i, pl.ds(0, 8, 2), :] + r["S1"][i, pl.ds(1, 8, 2), :]
            g = z_mean(s, 1)
            r["G2"][i] = g
            v2[i] = r["I2"][i] * g
            return 0

        lax.fori_loop(1, 7, start2, 0)

        def resid2(i):
            _, n = around(2, v2, i)
            return (1.0 - OMEGA) * r["G2"][i] + n

        first3 = []
        for a in (0, 1):
            t = resid2(2 * a + 2) + resid2(2 * a + 3)
            first3.append(inv3[a] * to_three(t))
        tile = jnp.zeros((8, 128), jnp.float32)
        for f, pair in ((0, first3), (1, [r["K3"][1], r["K3"][2]])):
            for a in (0, 1):
                moved = roll(pair[a], 4 * f + a - 2, 0)
                tile = jnp.where((row == 4 * f + a) | (row == 4 * f + a + 2), moved, tile)
        r["A"][cyc, R] = tile
        for d in far_first:
            pl.when(exists(0, d))(lambda d=d, c=cyc: z_copies(d, c, True).start())
        each(lambda i, c=cyc: side_copy(i, c, True).start())
        for d in STEPS:
            pl.when(exists(0, d))(lambda d=d, c=cyc: z_copies(d, c, False).wait_recv())
        packed = jnp.zeros((8, 128), jnp.float32)
        for s in range(2 * R + 1):
            packed = jnp.where(slot == s, r["A"][cyc, s], packed)
        r["B"][cyc, pl.ds(8 * R, 8)] = packed
        for d in far_first:
            pl.when(exists(d, 0))(lambda d=d, c=cyc: x_copies(d, c, True).start())

        each(lambda i, c=cyc: side_copy(i, c, False).wait_recv())
        low, high = row < 2, row >= 6

        def ring(xs, mid, ys_low, ys_high):
            return jnp.where(low, roll(ys_low, -4, 0), jnp.where(high, roll(ys_high, 4, 0), mid))

        for i in range(8):
            if i < 2:
                args = (r["SX"][cyc, 0, i], r["SC"][cyc, 0, i], r["SC"][cyc, 1, i])
            elif i < 6:
                args = (v2[i], r["SY"][cyc, 0, i - 2], r["SY"][cyc, 1, i - 2])
            else:
                args = (r["SX"][cyc, 1, i - 6], r["SC"][cyc, 2, i - 6], r["SC"][cyc, 3, i - 6])
            r["VF2"][i] = ring(None, *args)

        for d in STEPS:
            pl.when(exists(d, 0))(lambda d=d, c=cyc: x_copies(d, c, False).wait_recv())

        def got(f, b, a):
            return r["B"][cyc, pl.ds(4 * f + 2 * b + a, 8, 8), :]

        def sides(c, b, a):
            xp = c[b][1] if a == 0 else roll(c[b][0], -1, 0)
            xm = c[b][0] if a == 1 else roll(c[b][1], 1, 0)
            yp = c[1][a] if b == 0 else roll(c[0][a], -1, 1)
            ym = c[0][a] if b == 1 else roll(c[1][a], 1, 1)
            return xp, xm, yp, ym, roll(c[b][a], -8, 1), roll(c[b][a], 8, 1)

        if cyc == 0:
            k3 = [[got(1, b, a) for a in (0, 1)] for b in (0, 1)]
            coarse_w = {}
            for b in (0, 1):
                for a in (0, 1):
                    k = k3[b][a]
                    ns = list(sides(k3, b, a))
                    ns[4] = jnp.where(lane < 120, ns[4], 0.0)
                    ns[5] = jnp.where(lane >= 8, ns[5], 0.0)
                    ws = [scale3 * (k + n) for n in ns]
                    total = ws[0] + ws[1] + ws[2] + ws[3] + ws[4] + ws[5]
                    ok = k > 0.0
                    inv = jnp.where(ok, OMEGA / jnp.where(ok, total, 1.0), 0.0)
                    ws[4] = jnp.where(lane < 120, ws[4], 0.0)
                    ws[5] = jnp.where(lane >= 8, ws[5], 0.0)
                    base = 7 * (2 * b + a)
                    for j, w in enumerate(ws):
                        r["W"][base + j] = inv * w
        start = [[got(0, b, a) for a in (0, 1)] for b in (0, 1)]

        def coarse(_, flat):
            c = [[flat[0], flat[1]], [flat[2], flat[3]]]
            new = []
            for b in (0, 1):
                for a in (0, 1):
                    base = 7 * (2 * b + a)
                    v = start[b][a] + (1.0 - OMEGA) * c[b][a]
                    for j, n in enumerate(sides(c, b, a)):
                        v = v + r["W"][base + j] * n
                    new.append(v)
            return tuple(new)

        flat = (start[0][0], start[0][1], start[1][0], start[1][1])
        flat = lax.fori_loop(0, SWEEPS - 1, coarse, flat)

        cell = row // 2
        want = (lane & ~7) + (R - 1) + (cell + 1) // 2
        for i in range(4):
            s, a = R - 1 + (i + 1) // 2, (i + 1) % 2
            e0 = jnp.broadcast_to(flat[a][s : s + 1], (8, 128))
            e1 = jnp.broadcast_to(flat[2 + a][s : s + 1], (8, 128))
            e = jnp.take_along_axis(jnp.where(cell % 2 == 0, e1, e0), want, axis=1)
            r["VE2"][2 * i] = r["VF2"][2 * i] + e
            r["VE2"][2 * i + 1] = r["VF2"][2 * i + 1] + e

        def up2(i, _):
            v, n = around(2, r["VE2"], i)
            v = (1.0 - OMEGA) * v + r["VF2"][i] + r["I2"][i] * n
            r["S2"][i, pl.ds(0, 8, 2), :] = v
            r["S2"][i, pl.ds(1, 8, 2), :] = v
            return 0

        lax.fori_loop(1, 7, up2, 0)

        def add1(i, _):
            e = r["S2"][i]
            r["VE1"][2 * i] = r["V1"][2 * i] + e
            r["VE1"][2 * i + 1] = r["V1"][2 * i + 1] + e
            return 0

        lax.fori_loop(1, 7, add1, 0)

        def up1(i, _):
            v, n = around(1, r["VE1"], i)
            v = (1.0 - OMEGA) * v + r["V1"][i] + r["I1"][i] * n
            r["F1"][i, pl.ds(0, 16, 2), :] = v
            r["F1"][i, pl.ds(1, 16, 2), :] = v
            return 0

        lax.fori_loop(3, 13, up1, 0)

        def add0(i, _):
            e = r["F1"][i]
            r["VE"][2 * i] = r["V"][2 * i] + e
            r["VE"][2 * i + 1] = r["V"][2 * i + 1] + e
            return 0

        lax.fori_loop(3, 13, add0, 0)

        def up0(i, _, c=cyc):
            v, n = around(0, r["VE"], i)
            if c == 0:
                v = (1.0 - OMEGA) * v + r["V"][i] + r["I0"][i] * n
            else:
                v = (1.0 - OMEGA) * v + r["I0"][i] * (r["G"][i] + n)
            if c == CYCLES - 1:
                out[i - 8] = v[8:24]
            else:
                r["VB"][i, 8:24] = v[8:24]
                r["F0"][i - 8] = v[8:24]
            return 0

        lax.fori_loop(8, 24, up0, 0)
        if cyc < CYCLES - 1:
            send_halo(r["F0"], r["VB"], r["vs"], r["vr"])

    sent_halo(m_hbm, r["M"], r["ms"], r["mr"])
    sent_halo(g_hbm, r["G"], r["gs"], r["gr"])
    sent_halo(r["F0"], r["VB"], r["vs"], r["vr"])
    for cyc in range(CYCLES):
        each(lambda i, c=cyc: side_copy(i, c, True).wait_send())
        for d in STEPS:
            pl.when(exists(0, d))(lambda d=d, c=cyc: z_copies(d, c, True).wait_send())
            pl.when(exists(d, 0))(lambda d=d, c=cyc: x_copies(d, c, True).wait_send())


def scratch():
    f = jnp.float32

    def vm(*shape):
        return pltpu.VMEM(shape, f)

    a, b, c = vm(32, 32, 128), vm(16, 16, 128), vm(8, 8, 128)
    dma = pltpu.SemaphoreType.DMA
    nd, ns = len(DIRS), 2 * R + 1
    shapes = [a, pltpu.VMEM((32, 32, 128), jnp.int32)] + [a] * 11
    shapes += [vm(16, 32, 128), vm(8, 16, 128), vm(16, 16, 128)]
    shapes += [b] * 10 + [vm(8, 16, 128), vm(16, 32, 128)]
    shapes += [c, vm(CYCLES, 8, 8, 128)] + [c] * 9 + [vm(4, 8, 128)]
    shapes += [vm(CYCLES, 2, 2, 8, 128), vm(CYCLES, 2, 4, 8, 128), vm(CYCLES, 4, 2, 8, 128)]
    shapes += [vm(CYCLES, ns, 8, 128), vm(CYCLES, 64, 128), vm(28, 8, 128)]
    shapes += [dma((2,))] + [dma((nd,))] * 6 + [dma((CYCLES, nd))] * 2 + [dma((CYCLES, ns))] * 4
    return shapes


def local(right_side, material, conductivity):
    nx, ny = lax.axis_size("gx"), lax.axis_size("gy")
    return pl.pallas_call(
        functools.partial(kernel, nx, ny),
        out_shape=jax.ShapeDtypeStruct(right_side.shape, right_side.dtype),
        in_specs=[
            pl.BlockSpec(memory_space=pltpu.SMEM),
            pl.BlockSpec(memory_space=pl.ANY),
            pl.BlockSpec(memory_space=pl.ANY),
        ],
        out_specs=pl.BlockSpec(memory_space=pltpu.VMEM),
        scratch_shapes=scratch(),
        compiler_params=pltpu.CompilerParams(collective_id=0, has_side_effects=True),
        name="vcycles",
    )(conductivity, right_side, material)


def solution(mesh):
    return jax.shard_map(
        local,
        mesh=mesh,
        in_specs=(P("gx", "gy", None), P("gx", "gy", None), P()),
        out_specs=P("gx", "gy", None),
        check_vma=False,
    )
```

```python
import functools

import jax
import jax.numpy as jnp
from jax import lax
from jax.experimental import pallas as pl
from jax.experimental.pallas import tpu as pltpu
from jax.sharding import PartitionSpec as P

MESH = pl.DeviceIdType.MESH
CYCLES = 2
SWEEPS = 6
OMEGA = 0.8
NMAT = 16
H = 8
R = 3
DIRS = tuple((a, b) for a in (-1, 0, 1) for b in (-1, 0, 1) if (a, b) != (0, 0))


STEPS = tuple(range(-R, R + 1))
PARTNERS = tuple(
    sorted(
        ((a, b) for a in STEPS for b in STEPS if (a or b) and abs(a) + abs(b) <= R + 1),
        key=lambda d: -abs(d[0]) - 1.25 * abs(d[1]),
    )
)
G_CUT, V_CUT = 6, 7


def send_part(s, n=H):
    return {1: slice(16 - n, 16), -1: slice(0, n), 0: slice(0, 16)}[s]


def halo_part(s, n=H):
    return {1: slice(24, 24 + n), -1: slice(8 - n, 8), 0: slice(8, 24)}[s]


def roll(v, shift, axis):
    return pltpu.roll(v, shift % v.shape[axis], axis)


def iota(shape, axis):
    return lax.broadcasted_iota(jnp.int32, shape, axis)


def pair_swap(v, apart, axis):
    low = (iota(v.shape, axis) & apart) == 0
    return jnp.where(low, roll(v, -apart, axis), roll(v, apart, axis))


def kernel(nx, ny, cond, g_hbm, m_hbm, out, *refs):
    names = (
        "G", "M", "K0", "V", "VB", "VE", "I0", "T0", "X0", "Y0", "Z0", "S0", "F1",
        "K1", "V1", "G1", "VE1", "I1", "X1", "Y1", "Z1", "S1", "S2",
        "K2", "V2", "VF2", "VE2", "I2", "X2", "Y2", "Z2", "K3", "F0", "C", "W",
        "lsem", "send", "recv", "ready",
    )
    r = dict(zip(names, refs, strict=True))
    px, py = lax.axis_index("gx"), lax.axis_index("gy")
    xs = {d: lax.rem(px + (d + nx), nx) if d else px for d in STEPS}
    ys = {d: lax.rem(py + (d + ny), ny) if d else py for d in STEPS}

    def dev(a, b):
        return (xs[a], ys[b])

    def remote(src, dst, sem, a, b):
        return pltpu.make_async_remote_copy(
            src_ref=src, dst_ref=dst, send_sem=r["send"].at[sem], recv_sem=r["recv"].at[sem],
            device_id=dev(a, b), device_id_type=MESH,
        )

    own = (slice(8, 24), slice(8, 24))
    lg = pltpu.make_async_copy(g_hbm, r["G"].at[own], r["lsem"].at[0])
    lm = pltpu.make_async_copy(m_hbm, r["M"].at[own], r["lsem"].at[1])
    lm.start()
    lg.start()
    barrier = pltpu.get_barrier_semaphore()
    for a, b in DIRS:
        pl.semaphore_signal(barrier, inc=1, device_id=dev(a, b), device_id_type=MESH)
    lane = iota((8, 128), 1)
    row = iota((8, 128), 0)
    slot = lane & 7
    table = jnp.zeros((8, 128), jnp.float32)
    for i in range(NMAT):
        table = jnp.where(lane == i, cond[i], table)
    table32 = jnp.concatenate([table] * 4, 0)
    pl.semaphore_wait(barrier, len(DIRS))

    def send_halo(src, dst, sem, cut):
        for a, b in DIRS:
            n = cut if a and b else H
            remote(
                src.at[send_part(a, n), send_part(b)],
                dst.at[halo_part(-a, n), halo_part(-b)],
                sem, a, b,
            ).start()

    def all_halos(dst, cut):
        view = dst.at[0 : (512 + 4 * H * cut) // 32]
        sem = {"M": M_SEM, "G": G_SEM, "VB": V_SEM}
        for name in sem:
            if dst is r[name]:
                return remote(view, view, sem[name], 1, 0)
        raise ValueError

    def clear_edges(ref, value):
        full = functools.partial(jnp.full, fill_value=value, dtype=ref.dtype)

        @pl.when(px == 0)
        def _():
            ref[0:8] = full((8, 32, 128))

        @pl.when(px == nx - 1)
        def _():
            ref[24:32] = full((8, 32, 128))

        @pl.when(py == 0)
        def _():
            ref[:, 0:8] = full((32, 8, 128))

        @pl.when(py == ny - 1)
        def _():
            ref[:, 24:32] = full((32, 8, 128))

    send_halo(m_hbm, r["M"], M_SEM, H)
    send_halo(g_hbm, r["G"], G_SEM, G_CUT)
    lm.wait()
    all_halos(r["M"], H).wait_recv()
    for a, b in ((-1, 0), (1, 0), (0, -1), (0, 1)):
        pl.semaphore_signal(r["ready"], inc=1, device_id=dev(a, b), device_id_type=MESH)
    clear_edges(r["M"], NMAT)

    def planes(lo, hi, step, one):
        def body(j, _):
            done = []
            for q in range(step):
                done += one(lo + j * step + q)
            for ref, i, v in done:
                ref[i] = v
            return 0

        lax.fori_loop(0, (hi - lo) // step, body, 0)

    def unrolled(lo, hi, one):
        done = []
        for i in range(lo, hi):
            done += one(i)
        for ref, i, v in done:
            ref[i] = v

    def face_values(lv, i):
        scale = 0.5 * 0.25**lv
        step = 1 << lv
        k_ref = r[f"K{lv}"]
        k, kn = k_ref[i], k_ref[i + 1]
        ln = iota(k.shape, 1)
        below, above = ln < 128 - step, ln >= step
        ky = roll(k, -1, 0)
        kz = roll(k, -step, 1)
        s = 6.0 * k + (kn + k_ref[i - 1]) + (ky + roll(k, 1, 0))
        s = s + jnp.where(below, kz, 0.0) + jnp.where(above, roll(k, step, 1), 0.0)
        total = scale * s
        inside = k > 0.0
        inv = jnp.where(inside, OMEGA / jnp.where(inside, total, 1.0), 0.0)
        res = [
            (r[f"X{lv}"], i, scale * (k + kn)),
            (r[f"Y{lv}"], i, scale * (k + ky)),
            (r[f"Z{lv}"], i, jnp.where(below, scale * (k + kz), 0.0)),
            (r[f"I{lv}"], i, inv),
        ]
        if lv == 0:
            res.append((r["T0"], i, total))
        return res

    def around(lv, v_ref, i):
        step = 1 << lv
        v = v_ref[i]
        x, y, z = r[f"X{lv}"], r[f"Y{lv}"][i], r[f"Z{lv}"][i]
        n = x[i] * v_ref[i + 1] + x[i - 1] * v_ref[i - 1]
        n = n + (y * roll(v, -1, 0) + roll(y * v, 1, 0))
        return v, n + (z * roll(v, -step, 1) + roll(z * v, step, 1))

    def z_mean(s, lv):
        return 0.125 * (s + pair_swap(s, 1 << lv, 1))

    def y_pairs(ref, i, n):
        return ref[i, pl.ds(0, n, 2), :] + ref[i, pl.ds(1, n, 2), :]

    def to_three(t):
        return z_mean(t + pair_swap(t, 1, 0), 2)

    def look(i):
        k = [jnp.take_along_axis(table32, r["M"][2 * i + q], axis=1) for q in (0, 1)]
        return [(r["K0"], 2 * i, k[0]), (r["K0"], 2 * i + 1, k[1]), (r["S0"], i, k[0] + k[1])]

    planes(0, 16, 4, look)
    planes(0, 16, 8, lambda i: [(r["K1"], i, z_mean(y_pairs(r["S0"], i, 16), 0))])
    unrolled(0, 8, lambda i: [(r["S1"], i, r["K1"][2 * i] + r["K1"][2 * i + 1])])
    unrolled(0, 8, lambda i: [(r["K2"], i, z_mean(y_pairs(r["S1"], i, 8), 1))])
    unrolled(0, 4, lambda i: [(r["K3"], i, to_three(r["K2"][2 * i] + r["K2"][2 * i + 1]))])
    for lv, scale in ((0, 0.5), (1, 0.125), (2, 0.03125)):
        r[f"X{lv}"][0] = scale * (r[f"K{lv}"][0] + r[f"K{lv}"][1])
    planes(1, 31, 3, functools.partial(face_values, 0))
    planes(1, 15, 7, functools.partial(face_values, 1))
    unrolled(1, 7, functools.partial(face_values, 2))

    scale3 = 0.5 * 0.25**3
    z_up, z_down = lane < 120, lane >= 8
    inv3 = []
    for i in (1, 2):
        k = r["K3"][i]
        s = r["K3"][i - 1] + r["K3"][i + 1] + roll(k, 2, 0) + roll(k, -2, 0)
        s = s + jnp.where(z_up, roll(k, -8, 1), 0.0) + jnp.where(z_down, roll(k, 8, 1), 0.0)
        inv3.append(OMEGA / (scale3 * (6.0 * k + s)))

    lg.wait()
    all_halos(r["G"], G_CUT).wait_recv()
    planes(1, 31, 6, lambda i: [(r["V"], i, r["I0"][i] * r["G"][i])])

    far_x, far_y = row - R, slot - R
    here = (px + far_x >= 0) & (px + far_x < nx) & (py + far_y >= 0) & (py + far_y < ny)
    here = here & (far_x <= R) & (jnp.abs(far_x) + jnp.abs(far_y) <= R + 1)

    def side_copy(a, b, cyc):
        out_part = {1: slice(4, 6), -1: slice(2, 4), 0: slice(2, 6)}
        in_part = {1: slice(6, 8), -1: slice(0, 2), 0: slice(2, 6)}
        return remote(
            r["V2"].at[cyc, out_part[a], out_part[b]],
            r["VF2"].at[cyc, in_part[-a], in_part[-b]],
            S_SEM + cyc, a, b,
        )

    def row_of(a, b):
        return 8 * (b + R) + a + R

    for cyc in range(CYCLES):
        if cyc:
            all_halos(r["VB"], V_CUT).wait_recv()
            clear_edges(r["VB"], 0.0)

            def sweep(i):
                v, n = around(0, r["VB"], i)
                return [(r["V"], i, (1.0 - OMEGA) * v + r["I0"][i] * (r["G"][i] + n))]

            planes(1, 31, 3, sweep)

        def resid0(i, first=cyc == 0):
            v, n = around(0, r["V"], i)
            if first:
                return (1.0 - OMEGA) * r["G"][i] + n
            return r["G"][i] - r["T0"][i] * v + n

        planes(1, 15, 2, lambda i: [(r["S0"], i, resid0(2 * i) + resid0(2 * i + 1))])

        def start1(i):
            g = z_mean(y_pairs(r["S0"], i, 16), 0)
            return [(r["G1"], i, g), (r["V1"], i, r["I1"][i] * g)]

        planes(1, 15, 7, start1)

        def resid1(i):
            _, n = around(1, r["V1"], i)
            return (1.0 - OMEGA) * r["G1"][i] + n

        planes(1, 7, 3, lambda i: [(r["S1"], i, resid1(2 * i) + resid1(2 * i + 1))])
        v2 = r["V2"].at[cyc]
        g2 = {i: z_mean(y_pairs(r["S1"], i, 8), 1) for i in range(1, 7)}
        unrolled(1, 7, lambda i: [(v2, i, r["I2"][i] * g2[i])])

        def resid2(i):
            _, n = around(2, v2, i)
            return (1.0 - OMEGA) * g2[i] + n

        first3 = []
        for a in (0, 1):
            first3.append(inv3[a] * to_three(resid2(2 * a + 2) + resid2(2 * a + 3)))
        mine = jnp.zeros((8, 128), jnp.float32)
        for f, pair in ((0, first3), (1, [r["K3"][1], r["K3"][2]])):
            for a in (0, 1):
                for b in (0, 1):
                    mine = jnp.where(slot == 4 * f + 2 * b + a, roll(pair[a], -2 - 2 * b, 0), mine)
        near = r["C"].at[cyc]
        near[row_of(0, 0) : row_of(0, 0) + 1] = mine[0:1]
        if cyc == 0:
            pl.semaphore_wait(r["ready"], 4)
        for a, b in DIRS:
            side_copy(a, b, cyc).start()
        for a, b in PARTNERS:
            remote(
                near.at[row_of(0, 0) : row_of(0, 0) + 1],
                near.at[row_of(-a, -b) : row_of(-a, -b) + 1],
                C_SEM + cyc, a, b,
            ).start()

        rows = near.at[0 : len(PARTNERS)]
        remote(rows, rows, C_SEM + cyc, 1, 0).wait_recv()

        tiles = [near[8 * s : 8 * s + 8] for s in range(2 * R + 1)]

        def got(p):
            v = jnp.zeros((8, 128), jnp.float32)
            for s, t in enumerate(tiles):
                v = jnp.where(here & (slot == s), roll(t, s - p, 1), v)
            return v

        def sides(c, b, a):
            xp = c[b][1] if a == 0 else roll(c[b][0], -1, 0)
            xm = c[b][0] if a == 1 else roll(c[b][1], 1, 0)
            yp = c[1][a] if b == 0 else roll(c[0][a], -1, 1)
            ym = c[0][a] if b == 1 else roll(c[1][a], 1, 1)
            return xp, xm, yp, ym, roll(c[b][a], -8, 1), roll(c[b][a], 8, 1)

        if cyc == 0:
            k3 = [[got(4 + 2 * b + a) for a in (0, 1)] for b in (0, 1)]
            for b in (0, 1):
                for a in (0, 1):
                    k = k3[b][a]
                    ns = list(sides(k3, b, a))
                    ns[4] = jnp.where(z_up, ns[4], 0.0)
                    ns[5] = jnp.where(z_down, ns[5], 0.0)
                    ws = [scale3 * (k + n) for n in ns]
                    total = (ws[0] + ws[1]) + (ws[2] + ws[3]) + (ws[4] + ws[5])
                    ok = k > 0.0
                    inv = jnp.where(ok, OMEGA / jnp.where(ok, total, 1.0), 0.0)
                    ws[4] = jnp.where(z_up, ws[4], 0.0)
                    ws[5] = jnp.where(z_down, ws[5], 0.0)
                    for j, w in enumerate(ws):
                        r["W"][6 * (2 * b + a) + j] = inv * w
        start = [[got(2 * b + a) for a in (0, 1)] for b in (0, 1)]

        def coarse(_, flat):
            c = [[flat[0], flat[1]], [flat[2], flat[3]]]
            new = []
            for b in (0, 1):
                for a in (0, 1):
                    t = [r["W"][6 * (2 * b + a) + j] * n for j, n in enumerate(sides(c, b, a))]
                    v = start[b][a] + (1.0 - OMEGA) * c[b][a]
                    new.append((v + (t[0] + t[1])) + ((t[2] + t[3]) + (t[4] + t[5])))
            return tuple(new)

        flat = (start[0][0], start[0][1], start[1][0], start[1][1])
        flat = lax.fori_loop(0, SWEEPS - 1, coarse, flat)

        ring = r["VF2"].at[cyc]
        remote(ring.at[0:6], ring.at[0:6], S_SEM + cyc, 1, 0).wait_recv()
        cell = row // 2
        want = (lane & ~7) + (R - 1) + (cell + 1) // 2
        full2 = {}
        for i in range(8):
            v = ring[i]
            if 2 <= i < 6:
                v = jnp.where((row >= 2) & (row < 6), v2[i], v)
            full2[i] = jnp.where(r["K2"][i] > 0.0, v, 0.0)
        for i in range(4):
            s, a = R - 1 + (i + 1) // 2, (i + 1) % 2
            e0 = jnp.broadcast_to(flat[a][s : s + 1], (8, 128))
            e1 = jnp.broadcast_to(flat[2 + a][s : s + 1], (8, 128))
            e = jnp.take_along_axis(jnp.where(cell % 2 == 0, e1, e0), want, axis=1)
            r["VE2"][2 * i] = full2[2 * i] + e
            r["VE2"][2 * i + 1] = full2[2 * i + 1] + e

        up2 = {}
        for i in range(1, 7):
            v, n = around(2, r["VE2"], i)
            up2[i] = (1.0 - OMEGA) * v + full2[i] + r["I2"][i] * n
        for i in range(1, 7):
            r["S2"][i, pl.ds(0, 8, 2), :] = up2[i]
            r["S2"][i, pl.ds(1, 8, 2), :] = up2[i]

        unrolled(2, 14, lambda i: [(r["VE1"], i, r["V1"][i] + r["S2"][i // 2])])

        def up1(j, _):
            new = []
            for q in range(5):
                i = 3 + 5 * j + q
                v, n = around(1, r["VE1"], i)
                new.append((i, (1.0 - OMEGA) * v + r["V1"][i] + r["I1"][i] * n))
            for i, v in new:
                r["F1"][i, pl.ds(0, 16, 2), :] = v
                r["F1"][i, pl.ds(1, 16, 2), :] = v
            return 0

        lax.fori_loop(0, 2, up1, 0)

        def add0(i):
            e = r["F1"][i]
            return [(r["VE"], 2 * i + q, r["V"][2 * i + q] + e) for q in (0, 1)]

        planes(3, 13, 5, add0)

        def up0(i, c=cyc):
            v, n = around(0, r["VE"], i)
            if c == 0:
                v = (1.0 - OMEGA) * v + r["V"][i] + r["I0"][i] * n
            else:
                v = (1.0 - OMEGA) * v + r["I0"][i] * (r["G"][i] + n)
            v = v[8:24]
            if c == CYCLES - 1:
                return [(out, i - 8, v)]
            return [(r["VB"].at[:, 8:24], i, v), (r["F0"], i - 8, v)]

        planes(8, 24, 4, up0)
        if cyc < CYCLES - 1:
            send_halo(r["F0"], r["VB"], V_SEM, V_CUT)

    all_halos(r["M"], H).wait_send()
    all_halos(r["G"], G_CUT).wait_send()
    all_halos(r["VB"], V_CUT).wait_send()
    for cyc in range(CYCLES):
        ring = r["VF2"].at[cyc, 0:6]
        remote(ring, ring, S_SEM + cyc, 1, 0).wait_send()
        rows = r["C"].at[cyc, 0 : len(PARTNERS)]
        remote(rows, rows, C_SEM + cyc, 1, 0).wait_send()


M_SEM, G_SEM, V_SEM, S_SEM, C_SEM = 0, 1, 2, 3, 3 + CYCLES


def scratch():
    f = jnp.float32

    def vm(*shape):
        return pltpu.VMEM(shape, f)

    a, b, c = vm(32, 32, 128), vm(16, 16, 128), vm(8, 8, 128)
    dma = pltpu.SemaphoreType.DMA
    shapes = [a, pltpu.VMEM((32, 32, 128), jnp.int32)] + [a] * 9
    shapes += [vm(16, 32, 128)] * 2 + [b] * 8 + [vm(8, 16, 128)] * 2
    shapes += [c] + [vm(CYCLES, 8, 8, 128)] * 2 + [c] * 5 + [vm(4, 8, 128), b]
    shapes += [vm(CYCLES, 64, 128), vm(24, 8, 128)]
    sems = C_SEM + CYCLES
    return shapes + [dma((2,)), dma((sems,)), dma((sems,)), pltpu.SemaphoreType.REGULAR]


def local(right_side, material, conductivity):
    nx, ny = lax.axis_size("gx"), lax.axis_size("gy")
    return pl.pallas_call(
        functools.partial(kernel, nx, ny),
        out_shape=jax.ShapeDtypeStruct(right_side.shape, right_side.dtype),
        in_specs=[
            pl.BlockSpec(memory_space=pltpu.SMEM),
            pl.BlockSpec(memory_space=pl.ANY),
            pl.BlockSpec(memory_space=pl.ANY),
        ],
        out_specs=pl.BlockSpec(memory_space=pltpu.VMEM),
        scratch_shapes=scratch(),
        compiler_params=pltpu.CompilerParams(collective_id=0, has_side_effects=True),
        name="vcycles",
    )(conductivity, right_side, material)


def solution(mesh):
    return jax.shard_map(
        local,
        mesh=mesh,
        in_specs=(P("gx", "gy", None), P("gx", "gy", None), P()),
        out_specs=P("gx", "gy", None),
        check_vma=False,
    )
```

```python
import functools

import jax
import jax.numpy as jnp
from jax import lax
from jax.experimental import pallas as pl
from jax.experimental.pallas import tpu as pltpu
from jax.sharding import PartitionSpec as P

MESH = pl.DeviceIdType.MESH
CYCLES = 2
SWEEPS = 6
OMEGA = 0.8
NMAT = 16
H = 8
R = 3
DIRS = tuple((a, b) for a in (-1, 0, 1) for b in (-1, 0, 1) if (a, b) != (0, 0))


STEPS = tuple(range(-R, R + 1))
PARTNERS = tuple(
    sorted(
        ((a, b) for a in STEPS for b in STEPS if (a or b) and abs(a) + abs(b) <= R + 1),
        key=lambda d: -abs(d[0]) - 1.25 * abs(d[1]),
    )
)


def send_part(s, n=H):
    return {1: slice(16 - n, 16), -1: slice(0, n), 0: slice(0, 16)}[s]


def halo_part(s, n=H):
    return {1: slice(24, 24 + n), -1: slice(8 - n, 8), 0: slice(8, 24)}[s]


def roll(v, shift, axis):
    return pltpu.roll(v, shift % v.shape[axis], axis)


def iota(shape, axis):
    return lax.broadcasted_iota(jnp.int32, shape, axis)


def pair_swap(v, apart, axis):
    low = (iota(v.shape, axis) & apart) == 0
    return jnp.where(low, roll(v, -apart, axis), roll(v, apart, axis))


def kernel(nx, ny, cond, g_hbm, m_hbm, out, *refs):
    names = (
        "G", "M", "K0", "V", "VB", "VE", "I0", "T0", "X0", "Y0", "Z0", "S0", "F1",
        "K1", "V1", "G1", "VE1", "I1", "X1", "Y1", "Z1", "S1", "S2",
        "K2", "V2", "VF2", "VE2", "I2", "X2", "Y2", "Z2", "K3", "F0", "C", "W",
        "FM", "FZ", "MS", "GS", "VS", "RS", "CS", "lsem", "send", "recv", "ready",
    )
    r = dict(zip(names, refs, strict=True))
    px, py = lax.axis_index("gx"), lax.axis_index("gy")
    x_ok = {d: (px + d >= 0) & (px + d < nx) for d in STEPS}
    y_ok = {d: (py + d >= 0) & (py + d < ny) for d in STEPS}

    def exists(a, b):
        if a == 0:
            return y_ok[b]
        return x_ok[a] if b == 0 else x_ok[a] & y_ok[b]

    def remote(src, dst, sem, a, b):
        return pltpu.make_async_remote_copy(
            src_ref=src, dst_ref=dst, send_sem=r["send"].at[sem], recv_sem=r["recv"].at[sem],
            device_id=(px + a, py + b), device_id_type=MESH,
        )

    def push(src, dst, sem, a, b, hole, fill, spare):
        ok = exists(a, b)
        pl.when(ok)(lambda: remote(src, dst, sem, a, b).start())

        @pl.when(jnp.logical_not(ok))
        def _():
            pltpu.make_async_copy(fill, hole, r["recv"].at[sem]).start()
            pltpu.make_async_copy(fill, spare, r["send"].at[sem]).start()

    def tell(sem, sides):
        for a, b in sides:
            @pl.when(exists(a, b))
            def _(a=a, b=b):
                pl.semaphore_signal(sem, inc=1, device_id=(px + a, py + b), device_id_type=MESH)

    def count(sides):
        n = jnp.int32(0)
        for a, b in sides:
            n = n + jnp.where(exists(a, b), 1, 0)
        return n

    own = (slice(8, 24), slice(8, 24))
    lg = pltpu.make_async_copy(g_hbm, r["G"].at[own], r["lsem"].at[0])
    lm = pltpu.make_async_copy(m_hbm, r["M"].at[own], r["lsem"].at[1])
    lm.start()
    lg.start()
    barrier = pltpu.get_barrier_semaphore()
    tell(barrier, FOUR)
    r["FM"][...] = jnp.full((16, 16, 128), NMAT, jnp.int32)
    r["FZ"][...] = jnp.zeros((16, 16, 128), jnp.float32)
    lane = iota((8, 128), 1)
    row = iota((8, 128), 0)
    slot = lane & 7
    table = jnp.zeros((8, 128), jnp.float32)
    for i in range(NMAT):
        table = jnp.where(lane == i, cond[i], table)
    table32 = jnp.concatenate([table] * 4, 0)
    pl.semaphore_wait(barrier, count(FOUR))

    def send_faces(src, name, along_y):
        dst, fill, spare, sem = r[name], r[FILL[name]], r[SPARE[name]], SEM[name]
        for q in (1, -1):
            a, b = (0, q) if along_y else (q, 0)
            hole = (halo_part(a), halo_part(b))
            push(
                src.at[send_part(a), send_part(b)], dst.at[halo_part(-a), halo_part(-b)],
                sem if along_y else sem + 1, a, b,
                dst.at[hole], fill.at[0 : 8 if a else 16, 0 : 8 if b else 16], spare.at[hole],
            )

    def send_corners(name):
        dst, fill, spare, n = r[name], r[FILL[name]], r[SPARE[name]], CUT[name]
        for a in (1, -1):
            near_planes = slice(24 - n, 24) if a == 1 else slice(8, 8 + n)
            for b in (1, -1):
                hole = (halo_part(a, n), halo_part(b))
                push(
                    dst.at[near_planes, halo_part(b)], dst.at[halo_part(-a, n), halo_part(b)],
                    SEM[name] + 1, a, 0, dst.at[hole], fill.at[0:n, 0:8], spare.at[hole],
                )

    def y_faces(name):
        view = r[name].at[0:8]
        return remote(view, view, SEM[name], 1, 0)

    def the_rest(name):
        view = r[name].at[0 : 8 + CUT[name]]
        return remote(view, view, SEM[name] + 1, 1, 0)

    send_faces(m_hbm, "M", True)
    send_faces(m_hbm, "M", False)
    send_faces(g_hbm, "G", True)
    y_faces("M").wait_recv()
    send_corners("M")
    send_faces(g_hbm, "G", False)
    lm.wait()
    the_rest("M").wait_recv()
    tell(r["ready"], FOUR)

    def planes(lo, hi, step, one):
        def body(j, _):
            done = []
            for q in range(step):
                done += one(lo + j * step + q)
            for ref, i, v in done:
                ref[i] = v
            return 0

        lax.fori_loop(0, (hi - lo) // step, body, 0)

    def unrolled(lo, hi, one):
        done = []
        for i in range(lo, hi):
            done += one(i)
        for ref, i, v in done:
            ref[i] = v

    def face_values(lv, i):
        scale = 0.5 * 0.25**lv
        step = 1 << lv
        k_ref = r[f"K{lv}"]
        k, kn = k_ref[i], k_ref[i + 1]
        ln = iota(k.shape, 1)
        below, above = ln < 128 - step, ln >= step
        ky = roll(k, -1, 0)
        kz = roll(k, -step, 1)
        s = 6.0 * k + (kn + k_ref[i - 1]) + (ky + roll(k, 1, 0))
        s = s + jnp.where(below, kz, 0.0) + jnp.where(above, roll(k, step, 1), 0.0)
        total = scale * s
        inside = k > 0.0
        inv = jnp.where(inside, OMEGA / jnp.where(inside, total, 1.0), 0.0)
        res = [
            (r[f"X{lv}"], i, scale * (k + kn)),
            (r[f"Y{lv}"], i, scale * (k + ky)),
            (r[f"Z{lv}"], i, jnp.where(below, scale * (k + kz), 0.0)),
            (r[f"I{lv}"], i, inv),
        ]
        if lv == 0:
            res.append((r["T0"], i, total))
        return res

    def around(lv, v_ref, i):
        step = 1 << lv
        v = v_ref[i]
        x, y, z = r[f"X{lv}"], r[f"Y{lv}"][i], r[f"Z{lv}"][i]
        n = x[i] * v_ref[i + 1] + x[i - 1] * v_ref[i - 1]
        n = n + (y * roll(v, -1, 0) + roll(y * v, 1, 0))
        return v, n + (z * roll(v, -step, 1) + roll(z * v, step, 1))

    def z_mean(s, lv):
        return 0.125 * (s + pair_swap(s, 1 << lv, 1))

    def y_pairs(ref, i, n):
        return ref[i, pl.ds(0, n, 2), :] + ref[i, pl.ds(1, n, 2), :]

    def to_three(t):
        return z_mean(t + pair_swap(t, 1, 0), 2)

    def look(i):
        k = [jnp.take_along_axis(table32, r["M"][2 * i + q], axis=1) for q in (0, 1)]
        return [(r["K0"], 2 * i, k[0]), (r["K0"], 2 * i + 1, k[1]), (r["S0"], i, k[0] + k[1])]

    planes(0, 16, 4, look)
    planes(0, 16, 8, lambda i: [(r["K1"], i, z_mean(y_pairs(r["S0"], i, 16), 0))])
    unrolled(0, 8, lambda i: [(r["S1"], i, r["K1"][2 * i] + r["K1"][2 * i + 1])])
    unrolled(0, 8, lambda i: [(r["K2"], i, z_mean(y_pairs(r["S1"], i, 8), 1))])
    unrolled(0, 4, lambda i: [(r["K3"], i, to_three(r["K2"][2 * i] + r["K2"][2 * i + 1]))])
    for lv, scale in ((0, 0.5), (1, 0.125), (2, 0.03125)):
        r[f"X{lv}"][0] = scale * (r[f"K{lv}"][0] + r[f"K{lv}"][1])
    y_faces("G").wait_recv()
    send_corners("G")
    planes(1, 31, 3, functools.partial(face_values, 0))
    planes(1, 15, 7, functools.partial(face_values, 1))
    unrolled(1, 7, functools.partial(face_values, 2))

    scale3 = 0.5 * 0.25**3
    z_up, z_down = lane < 120, lane >= 8
    inv3 = []
    for i in (1, 2):
        k = r["K3"][i]
        s = r["K3"][i - 1] + r["K3"][i + 1] + roll(k, 2, 0) + roll(k, -2, 0)
        s = s + jnp.where(z_up, roll(k, -8, 1), 0.0) + jnp.where(z_down, roll(k, 8, 1), 0.0)
        inv3.append(OMEGA / (scale3 * (6.0 * k + s)))

    lg.wait()
    the_rest("G").wait_recv()
    planes(1, 31, 6, lambda i: [(r["V"], i, r["I0"][i] * r["G"][i])])

    far_x, far_y = row - R, slot - R
    here = (px + far_x >= 0) & (px + far_x < nx) & (py + far_y >= 0) & (py + far_y < ny)
    here = here & (far_x <= R) & (jnp.abs(far_x) + jnp.abs(far_y) <= R + 1)

    def side_copy(a, b, cyc):
        out_part = {1: slice(4, 6), -1: slice(2, 4), 0: slice(2, 6)}
        in_part = {1: slice(6, 8), -1: slice(0, 2), 0: slice(2, 6)}
        src, hole = (cyc, out_part[a], out_part[b]), (cyc, in_part[a], in_part[b])
        push(
            r["V2"].at[src], r["VF2"].at[cyc, in_part[-a], in_part[-b]], S_SEM + cyc, a, b,
            r["VF2"].at[hole], r["V2"].at[src], r["RS"].at[hole],
        )

    def row_of(a, b):
        return 8 * (b + R) + a + R

    for cyc in range(CYCLES):
        if cyc:
            y_faces("VB").wait_recv()
            send_corners("VB")
            the_rest("VB").wait_recv()

            def sweep(i):
                v, n = around(0, r["VB"], i)
                return [(r["V"], i, (1.0 - OMEGA) * v + r["I0"][i] * (r["G"][i] + n))]

            planes(1, 31, 3, sweep)

        def resid0(i, first=cyc == 0):
            v, n = around(0, r["V"], i)
            if first:
                return (1.0 - OMEGA) * r["G"][i] + n
            return r["G"][i] - r["T0"][i] * v + n

        planes(1, 15, 2, lambda i: [(r["S0"], i, resid0(2 * i) + resid0(2 * i + 1))])

        def start1(i):
            g = z_mean(y_pairs(r["S0"], i, 16), 0)
            return [(r["G1"], i, g), (r["V1"], i, r["I1"][i] * g)]

        planes(1, 15, 7, start1)

        def resid1(i):
            _, n = around(1, r["V1"], i)
            return (1.0 - OMEGA) * r["G1"][i] + n

        planes(1, 7, 3, lambda i: [(r["S1"], i, resid1(2 * i) + resid1(2 * i + 1))])
        v2 = r["V2"].at[cyc]
        g2 = {i: z_mean(y_pairs(r["S1"], i, 8), 1) for i in range(1, 7)}
        unrolled(1, 7, lambda i: [(v2, i, r["I2"][i] * g2[i])])

        def resid2(i):
            _, n = around(2, v2, i)
            return (1.0 - OMEGA) * g2[i] + n

        first3 = []
        for a in (0, 1):
            first3.append(inv3[a] * to_three(resid2(2 * a + 2) + resid2(2 * a + 3)))
        mine = jnp.zeros((8, 128), jnp.float32)
        for f, pair in ((0, first3), (1, [r["K3"][1], r["K3"][2]])):
            for a in (0, 1):
                for b in (0, 1):
                    mine = jnp.where(slot == 4 * f + 2 * b + a, roll(pair[a], -2 - 2 * b, 0), mine)
        near = r["C"].at[cyc]
        near[row_of(0, 0) : row_of(0, 0) + 1] = mine[0:1]
        if cyc == 0:
            pl.semaphore_wait(r["ready"], count(FOUR))
        for a, b in DIRS:
            side_copy(a, b, cyc)
        my_row = near.at[row_of(0, 0) : row_of(0, 0) + 1]
        for a, b in PARTNERS:
            there, hole = row_of(-a, -b), row_of(a, b)
            push(
                my_row, near.at[there : there + 1], C_SEM + cyc, a, b,
                near.at[hole : hole + 1], my_row, r["CS"].at[cyc, hole : hole + 1],
            )

        rows = near.at[0 : len(PARTNERS)]
        remote(rows, rows, C_SEM + cyc, 1, 0).wait_recv()

        tiles = [near[8 * s : 8 * s + 8] for s in range(2 * R + 1)]

        def got(p):
            v = jnp.zeros((8, 128), jnp.float32)
            for s, t in enumerate(tiles):
                v = jnp.where(here & (slot == s), roll(t, s - p, 1), v)
            return v

        def sides(c, b, a):
            xp = c[b][1] if a == 0 else roll(c[b][0], -1, 0)
            xm = c[b][0] if a == 1 else roll(c[b][1], 1, 0)
            yp = c[1][a] if b == 0 else roll(c[0][a], -1, 1)
            ym = c[0][a] if b == 1 else roll(c[1][a], 1, 1)
            return xp, xm, yp, ym, roll(c[b][a], -8, 1), roll(c[b][a], 8, 1)

        if cyc == 0:
            k3 = [[got(4 + 2 * b + a) for a in (0, 1)] for b in (0, 1)]
            for b in (0, 1):
                for a in (0, 1):
                    k = k3[b][a]
                    ns = list(sides(k3, b, a))
                    ns[4] = jnp.where(z_up, ns[4], 0.0)
                    ns[5] = jnp.where(z_down, ns[5], 0.0)
                    ws = [scale3 * (k + n) for n in ns]
                    total = (ws[0] + ws[1]) + (ws[2] + ws[3]) + (ws[4] + ws[5])
                    ok = k > 0.0
                    inv = jnp.where(ok, OMEGA / jnp.where(ok, total, 1.0), 0.0)
                    ws[4] = jnp.where(z_up, ws[4], 0.0)
                    ws[5] = jnp.where(z_down, ws[5], 0.0)
                    for j, w in enumerate(ws):
                        r["W"][6 * (2 * b + a) + j] = inv * w
        start = [[got(2 * b + a) for a in (0, 1)] for b in (0, 1)]

        def coarse(_, flat):
            c = [[flat[0], flat[1]], [flat[2], flat[3]]]
            new = []
            for b in (0, 1):
                for a in (0, 1):
                    t = [r["W"][6 * (2 * b + a) + j] * n for j, n in enumerate(sides(c, b, a))]
                    v = start[b][a] + (1.0 - OMEGA) * c[b][a]
                    new.append((v + (t[0] + t[1])) + ((t[2] + t[3]) + (t[4] + t[5])))
            return tuple(new)

        flat = (start[0][0], start[0][1], start[1][0], start[1][1])
        flat = lax.fori_loop(0, SWEEPS - 1, coarse, flat)

        ring = r["VF2"].at[cyc]
        remote(ring.at[0:6], ring.at[0:6], S_SEM + cyc, 1, 0).wait_recv()
        cell = row // 2
        want = (lane & ~7) + (R - 1) + (cell + 1) // 2
        full2 = {}
        for i in range(8):
            v = ring[i]
            if 2 <= i < 6:
                v = jnp.where((row >= 2) & (row < 6), v2[i], v)
            full2[i] = jnp.where(r["K2"][i] > 0.0, v, 0.0)
        for i in range(4):
            s, a = R - 1 + (i + 1) // 2, (i + 1) % 2
            e0 = jnp.broadcast_to(flat[a][s : s + 1], (8, 128))
            e1 = jnp.broadcast_to(flat[2 + a][s : s + 1], (8, 128))
            e = jnp.take_along_axis(jnp.where(cell % 2 == 0, e1, e0), want, axis=1)
            r["VE2"][2 * i] = full2[2 * i] + e
            r["VE2"][2 * i + 1] = full2[2 * i + 1] + e

        up2 = {}
        for i in range(1, 7):
            v, n = around(2, r["VE2"], i)
            up2[i] = (1.0 - OMEGA) * v + full2[i] + r["I2"][i] * n
        for i in range(1, 7):
            r["S2"][i, pl.ds(0, 8, 2), :] = up2[i]
            r["S2"][i, pl.ds(1, 8, 2), :] = up2[i]

        unrolled(2, 14, lambda i: [(r["VE1"], i, r["V1"][i] + r["S2"][i // 2])])

        def up1(j, _):
            new = []
            for q in range(5):
                i = 3 + 5 * j + q
                v, n = around(1, r["VE1"], i)
                new.append((i, (1.0 - OMEGA) * v + r["V1"][i] + r["I1"][i] * n))
            for i, v in new:
                r["F1"][i, pl.ds(0, 16, 2), :] = v
                r["F1"][i, pl.ds(1, 16, 2), :] = v
            return 0

        lax.fori_loop(0, 2, up1, 0)

        def add0(i):
            e = r["F1"][i]
            return [(r["VE"], 2 * i + q, r["V"][2 * i + q] + e) for q in (0, 1)]

        planes(3, 13, 5, add0)

        def up0(i, c=cyc):
            v, n = around(0, r["VE"], i)
            if c == 0:
                v = (1.0 - OMEGA) * v + r["V"][i] + r["I0"][i] * n
            else:
                v = (1.0 - OMEGA) * v + r["I0"][i] * (r["G"][i] + n)
            v = v[8:24]
            if c == CYCLES - 1:
                return [(out, i - 8, v)]
            return [(r["VB"].at[:, 8:24], i, v), (r["F0"], i - 8, v)]

        planes(8, 24, 4, up0)
        if cyc < CYCLES - 1:
            send_faces(r["F0"], "VB", True)
            send_faces(r["F0"], "VB", False)

    for name in SEM:
        y_faces(name).wait_send()
        the_rest(name).wait_send()
    for cyc in range(CYCLES):
        ring = r["VF2"].at[cyc, 0:6]
        remote(ring, ring, S_SEM + cyc, 1, 0).wait_send()
        rows = r["C"].at[cyc, 0 : len(PARTNERS)]
        remote(rows, rows, C_SEM + cyc, 1, 0).wait_send()


SEM = {"M": 0, "G": 2, "VB": 4}
S_SEM, C_SEM = 6, 6 + CYCLES
CUT = {"M": 8, "G": 6, "VB": 7}
FILL = {"M": "FM", "G": "FZ", "VB": "FZ"}
SPARE = {"M": "MS", "G": "GS", "VB": "VS"}
FOUR = ((1, 0), (-1, 0), (0, 1), (0, -1))


def scratch():
    f = jnp.float32

    def vm(*shape):
        return pltpu.VMEM(shape, f)

    a, b, c = vm(32, 32, 128), vm(16, 16, 128), vm(8, 8, 128)
    dma = pltpu.SemaphoreType.DMA
    shapes = [a, pltpu.VMEM((32, 32, 128), jnp.int32)] + [a] * 9
    shapes += [vm(16, 32, 128)] * 2 + [b] * 8 + [vm(8, 16, 128)] * 2
    shapes += [c] + [vm(CYCLES, 8, 8, 128)] * 2 + [c] * 5 + [vm(4, 8, 128), b]
    shapes += [vm(CYCLES, 64, 128), vm(24, 8, 128)]
    sems = C_SEM + CYCLES
    i16, i32 = (pltpu.VMEM((n, n, 128), jnp.int32) for n in (16, 32))
    shapes += [i16, b, i32, a, a, vm(CYCLES, 8, 8, 128), vm(CYCLES, 64, 128)]
    return shapes + [dma((2,)), dma((sems,)), dma((sems,)), pltpu.SemaphoreType.REGULAR]


def local(right_side, material, conductivity):
    nx, ny = lax.axis_size("gx"), lax.axis_size("gy")
    return pl.pallas_call(
        functools.partial(kernel, nx, ny),
        out_shape=jax.ShapeDtypeStruct(right_side.shape, right_side.dtype),
        in_specs=[
            pl.BlockSpec(memory_space=pltpu.SMEM),
            pl.BlockSpec(memory_space=pl.ANY),
            pl.BlockSpec(memory_space=pl.ANY),
        ],
        out_specs=pl.BlockSpec(memory_space=pltpu.VMEM),
        scratch_shapes=scratch(),
        compiler_params=pltpu.CompilerParams(collective_id=0, has_side_effects=True),
        name="vcycles",
    )(conductivity, right_side, material)


def solution(mesh):
    return jax.shard_map(
        local,
        mesh=mesh,
        in_specs=(P("gx", "gy", None), P("gx", "gy", None), P()),
        out_specs=P("gx", "gy", None),
        check_vma=False,
    )
```

```python
import functools

import jax
import jax.numpy as jnp
from jax import lax
from jax.experimental import pallas as pl
from jax.experimental.pallas import tpu as pltpu
from jax.sharding import PartitionSpec as P

MESH = pl.DeviceIdType.MESH
CYCLES = 2
SWEEPS = 6
OMEGA = 0.8
NMAT = 16
H = 8
R = 3
DIRS = tuple((a, b) for a in (-1, 0, 1) for b in (-1, 0, 1) if (a, b) != (0, 0))


STEPS = tuple(range(-R, R + 1))
PARTNERS = tuple(
    sorted(
        ((a, b) for a in STEPS for b in STEPS if (a or b) and abs(a) + abs(b) <= R + 1),
        key=lambda d: -abs(d[0]) - 1.25 * abs(d[1]),
    )
)


def send_part(s, n=H):
    return {1: slice(16 - n, 16), -1: slice(0, n), 0: slice(0, 16)}[s]


def halo_part(s, n=H):
    return {1: slice(24, 24 + n), -1: slice(8 - n, 8), 0: slice(8, 24)}[s]


def roll(v, shift, axis):
    return pltpu.roll(v, shift % v.shape[axis], axis)


def iota(shape, axis):
    return lax.broadcasted_iota(jnp.int32, shape, axis)


def pair_swap(v, apart, axis):
    low = (iota(v.shape, axis) & apart) == 0
    return jnp.where(low, roll(v, -apart, axis), roll(v, apart, axis))


def kernel(nx, ny, cond, g_hbm, m_hbm, out, *refs):
    names = (
        "G", "M", "K0", "V", "VB", "VE", "I0", "T0", "X0", "Y0", "Z0", "S0", "F1",
        "K1", "V1", "G1", "VE1", "I1", "X1", "Y1", "Z1", "S1", "S2",
        "K2", "V2", "VF2", "VE2", "I2", "X2", "Y2", "Z2", "K3", "F0", "C", "W",
        "FM", "FZ", "MS", "GS", "VS", "lsem", "send", "recv", "ready",
    )
    r = dict(zip(names, refs, strict=True))
    px, py = lax.axis_index("gx"), lax.axis_index("gy")
    x_ok = {d: (px + d >= 0) & (px + d < nx) for d in STEPS}
    y_ok = {d: (py + d >= 0) & (py + d < ny) for d in STEPS}

    xs = {d: lax.rem(px + (d + nx), nx) if d else px for d in STEPS}
    ys = {d: lax.rem(py + (d + ny), ny) if d else py for d in STEPS}

    def exists(a, b):
        if a == 0:
            return y_ok[b]
        return x_ok[a] if b == 0 else x_ok[a] & y_ok[b]

    def remote(src, dst, sem, a, b):
        return pltpu.make_async_remote_copy(
            src_ref=src, dst_ref=dst, send_sem=r["send"].at[sem], recv_sem=r["recv"].at[sem],
            device_id=(xs[a], ys[b]), device_id_type=MESH,
        )

    def push(src, dst, sem, a, b, hole, fill, spare):
        ok = exists(a, b)
        pl.when(ok)(lambda: remote(src, dst, sem, a, b).start())

        @pl.when(jnp.logical_not(ok))
        def _():
            pltpu.make_async_copy(fill, hole, r["recv"].at[sem]).start()
            pltpu.make_async_copy(fill, spare, r["send"].at[sem]).start()

    def tell(sem):
        for a, b in FOUR:
            pl.semaphore_signal(sem, inc=1, device_id=(xs[a], ys[b]), device_id_type=MESH)

    own = (slice(8, 24), slice(8, 24))
    lg = pltpu.make_async_copy(g_hbm, r["G"].at[own], r["lsem"].at[0])
    lm = pltpu.make_async_copy(m_hbm, r["M"].at[own], r["lsem"].at[1])
    lm.start()
    lg.start()
    barrier = pltpu.get_barrier_semaphore()
    tell(barrier)
    r["FM"][...] = jnp.full((16, 16, 128), NMAT, jnp.int32)
    r["FZ"][...] = jnp.zeros((16, 16, 128), jnp.float32)
    lane = iota((8, 128), 1)
    row = iota((8, 128), 0)
    slot = lane & 7
    table = jnp.zeros((8, 128), jnp.float32)
    for i in range(NMAT):
        table = jnp.where(lane == i, cond[i], table)
    table32 = jnp.concatenate([table] * 4, 0)
    pl.semaphore_wait(barrier, 4)
    tell(r["ready"].at[0])

    def send_faces(src, name, along_y):
        dst, fill, spare, sem = r[name], r[FILL[name]], r[SPARE[name]], SEM[name]
        for q in (1, -1):
            a, b = (0, q) if along_y else (q, 0)
            hole = (halo_part(a), halo_part(b))
            push(
                src.at[send_part(a), send_part(b)], dst.at[halo_part(-a), halo_part(-b)],
                sem if along_y else sem + 1, a, b,
                dst.at[hole], fill.at[0 : 8 if a else 16, 0 : 8 if b else 16], spare.at[hole],
            )

    def send_corners(name):
        dst, fill, spare, n = r[name], r[FILL[name]], r[SPARE[name]], CUT[name]
        for a in (1, -1):
            near_planes = slice(24 - n, 24) if a == 1 else slice(8, 8 + n)
            for b in (1, -1):
                hole = (halo_part(a, n), halo_part(b))
                push(
                    dst.at[near_planes, halo_part(b)], dst.at[halo_part(-a, n), halo_part(b)],
                    SEM[name] + 1, a, 0, dst.at[hole], fill.at[0:n, 0:8], spare.at[hole],
                )

    def send_field():
        dst, n = r["VB"], CUT["VB"]
        for a, b in sorted(DIRS, key=lambda d: -abs(d[0]) - abs(d[1])):
            m = n if a and b else H
            hole = (halo_part(a, m), halo_part(b))
            tall, wide = m if a else 16, 8 if b else 16
            push(
                r["F0"].at[send_part(a, m), send_part(b)],
                dst.at[halo_part(-a, m), halo_part(-b)], V_SEM, a, b,
                dst.at[hole], r["FZ"].at[0:tall, 0:wide], r["VS"].at[hole],
            )

    def field():
        view = r["VB"].at[0 : 16 + CUT["VB"]]
        return remote(view, view, V_SEM, 1, 0)

    def y_faces(name):
        view = r[name].at[0:8]
        return remote(view, view, SEM[name], 1, 0)

    def the_rest(name):
        view = r[name].at[0 : 8 + CUT[name]]
        return remote(view, view, SEM[name] + 1, 1, 0)

    send_faces(m_hbm, "M", True)
    send_faces(m_hbm, "M", False)
    send_faces(g_hbm, "G", True)
    y_faces("M").wait_recv()
    send_corners("M")
    send_faces(g_hbm, "G", False)
    pl.semaphore_wait(r["ready"].at[0], 4)
    tell(r["ready"].at[1])
    lm.wait()
    the_rest("M").wait_recv()
    pl.semaphore_wait(r["ready"].at[1], 4)
    tell(r["ready"].at[2])

    def planes(lo, hi, step, one):
        def body(j, _):
            done = []
            for q in range(step):
                done += one(lo + j * step + q)
            for ref, i, v in done:
                ref[i] = v
            return 0

        lax.fori_loop(0, (hi - lo) // step, body, 0)

    def unrolled(lo, hi, one):
        done = []
        for i in range(lo, hi):
            done += one(i)
        for ref, i, v in done:
            ref[i] = v

    def face_values(lv, i):
        scale = 0.5 * 0.25**lv
        step = 1 << lv
        k_ref = r[f"K{lv}"]
        k, kn = k_ref[i], k_ref[i + 1]
        ln = iota(k.shape, 1)
        below, above = ln < 128 - step, ln >= step
        ky = roll(k, -1, 0)
        kz = roll(k, -step, 1)
        s = 6.0 * k + (kn + k_ref[i - 1]) + (ky + roll(k, 1, 0))
        s = s + jnp.where(below, kz, 0.0) + jnp.where(above, roll(k, step, 1), 0.0)
        total = scale * s
        inside = k > 0.0
        inv = jnp.where(inside, OMEGA / jnp.where(inside, total, 1.0), 0.0)
        res = [
            (r[f"X{lv}"], i, scale * (k + kn)),
            (r[f"Y{lv}"], i, scale * (k + ky)),
            (r[f"Z{lv}"], i, jnp.where(below, scale * (k + kz), 0.0)),
            (r[f"I{lv}"], i, inv),
        ]
        if lv == 0:
            res.append((r["T0"], i, total))
        return res

    def around(lv, v_ref, i):
        step = 1 << lv
        v = v_ref[i]
        x, y, z = r[f"X{lv}"], r[f"Y{lv}"][i], r[f"Z{lv}"][i]
        n = x[i] * v_ref[i + 1] + x[i - 1] * v_ref[i - 1]
        n = n + (y * roll(v, -1, 0) + roll(y * v, 1, 0))
        return v, n + (z * roll(v, -step, 1) + roll(z * v, step, 1))

    def z_mean(s, lv):
        return 0.125 * (s + pair_swap(s, 1 << lv, 1))

    def y_pairs(ref, i, n):
        return ref[i, pl.ds(0, n, 2), :] + ref[i, pl.ds(1, n, 2), :]

    def to_three(t):
        return z_mean(t + pair_swap(t, 1, 0), 2)

    def look(i):
        k = [jnp.take_along_axis(table32, r["M"][2 * i + q], axis=1) for q in (0, 1)]
        return [(r["K0"], 2 * i, k[0]), (r["K0"], 2 * i + 1, k[1]), (r["S0"], i, k[0] + k[1])]

    planes(0, 16, 4, look)
    planes(0, 16, 8, lambda i: [(r["K1"], i, z_mean(y_pairs(r["S0"], i, 16), 0))])
    unrolled(0, 8, lambda i: [(r["S1"], i, r["K1"][2 * i] + r["K1"][2 * i + 1])])
    unrolled(0, 8, lambda i: [(r["K2"], i, z_mean(y_pairs(r["S1"], i, 8), 1))])
    unrolled(0, 4, lambda i: [(r["K3"], i, to_three(r["K2"][2 * i] + r["K2"][2 * i + 1]))])
    for lv, scale in ((0, 0.5), (1, 0.125), (2, 0.03125)):
        r[f"X{lv}"][0] = scale * (r[f"K{lv}"][0] + r[f"K{lv}"][1])
    y_faces("G").wait_recv()
    send_corners("G")
    planes(1, 31, 3, functools.partial(face_values, 0))
    planes(1, 15, 7, functools.partial(face_values, 1))
    unrolled(1, 7, functools.partial(face_values, 2))

    scale3 = 0.5 * 0.25**3
    z_up, z_down = lane < 120, lane >= 8
    inv3 = []
    for i in (1, 2):
        k = r["K3"][i]
        s = r["K3"][i - 1] + r["K3"][i + 1] + roll(k, 2, 0) + roll(k, -2, 0)
        s = s + jnp.where(z_up, roll(k, -8, 1), 0.0) + jnp.where(z_down, roll(k, 8, 1), 0.0)
        inv3.append(OMEGA / (scale3 * (6.0 * k + s)))

    lg.wait()
    the_rest("G").wait_recv()
    planes(1, 31, 6, lambda i: [(r["V"], i, r["I0"][i] * r["G"][i])])

    far_x, far_y = row - R, slot - R
    here = (px + far_x >= 0) & (px + far_x < nx) & (py + far_y >= 0) & (py + far_y < ny)
    here = here & (far_x <= R) & (jnp.abs(far_x) + jnp.abs(far_y) <= R + 1)

    def side_copy(a, b, cyc):
        out_part = {1: slice(4, 6), -1: slice(2, 4), 0: slice(2, 6)}
        in_part = {1: slice(6, 8), -1: slice(0, 2), 0: slice(2, 6)}
        return remote(
            r["V2"].at[cyc, out_part[a], out_part[b]],
            r["VF2"].at[cyc, in_part[-a], in_part[-b]],
            S_SEM + cyc, a, b,
        )

    def row_of(a, b):
        return 8 * (b + R) + a + R

    for cyc in range(CYCLES):
        if cyc:
            field().wait_recv()

            def sweep(i):
                v, n = around(0, r["VB"], i)
                return [(r["V"], i, (1.0 - OMEGA) * v + r["I0"][i] * (r["G"][i] + n))]

            planes(1, 31, 3, sweep)

        def resid0(i, first=cyc == 0):
            v, n = around(0, r["V"], i)
            if first:
                return (1.0 - OMEGA) * r["G"][i] + n
            return r["G"][i] - r["T0"][i] * v + n

        planes(1, 15, 2, lambda i: [(r["S0"], i, resid0(2 * i) + resid0(2 * i + 1))])

        def start1(i):
            g = z_mean(y_pairs(r["S0"], i, 16), 0)
            return [(r["G1"], i, g), (r["V1"], i, r["I1"][i] * g)]

        planes(1, 15, 7, start1)

        def resid1(i):
            _, n = around(1, r["V1"], i)
            return (1.0 - OMEGA) * r["G1"][i] + n

        planes(1, 7, 3, lambda i: [(r["S1"], i, resid1(2 * i) + resid1(2 * i + 1))])
        v2 = r["V2"].at[cyc]
        g2 = {i: z_mean(y_pairs(r["S1"], i, 8), 1) for i in range(1, 7)}
        unrolled(1, 7, lambda i: [(v2, i, r["I2"][i] * g2[i])])

        def resid2(i):
            _, n = around(2, v2, i)
            return (1.0 - OMEGA) * g2[i] + n

        first3 = []
        for a in (0, 1):
            first3.append(inv3[a] * to_three(resid2(2 * a + 2) + resid2(2 * a + 3)))
        mine = jnp.zeros((8, 128), jnp.float32)
        for f, pair in ((0, first3), (1, [r["K3"][1], r["K3"][2]])):
            for a in (0, 1):
                for b in (0, 1):
                    mine = jnp.where(slot == 4 * f + 2 * b + a, roll(pair[a], -2 - 2 * b, 0), mine)
        near = r["C"].at[cyc]
        near[row_of(0, 0) : row_of(0, 0) + 1] = mine[0:1]
        if cyc == 0:
            pl.semaphore_wait(r["ready"].at[2], 4)
        for a, b in DIRS:
            side_copy(a, b, cyc).start()
        my_row = near.at[row_of(0, 0) : row_of(0, 0) + 1]
        for a, b in PARTNERS:
            there = row_of(-a, -b)
            remote(my_row, near.at[there : there + 1], C_SEM + cyc, a, b).start()

        rows = near.at[0 : len(PARTNERS)]
        remote(rows, rows, C_SEM + cyc, 1, 0).wait_recv()

        tiles = [near[8 * s : 8 * s + 8] for s in range(2 * R + 1)]

        def got(p):
            v = jnp.zeros((8, 128), jnp.float32)
            for s, t in enumerate(tiles):
                v = jnp.where(here & (slot == s), roll(t, s - p, 1), v)
            return v

        def sides(c, b, a):
            xp = c[b][1] if a == 0 else roll(c[b][0], -1, 0)
            xm = c[b][0] if a == 1 else roll(c[b][1], 1, 0)
            yp = c[1][a] if b == 0 else roll(c[0][a], -1, 1)
            ym = c[0][a] if b == 1 else roll(c[1][a], 1, 1)
            return xp, xm, yp, ym, roll(c[b][a], -8, 1), roll(c[b][a], 8, 1)

        if cyc == 0:
            k3 = [[got(4 + 2 * b + a) for a in (0, 1)] for b in (0, 1)]
            for b in (0, 1):
                for a in (0, 1):
                    k = k3[b][a]
                    ns = list(sides(k3, b, a))
                    ns[4] = jnp.where(z_up, ns[4], 0.0)
                    ns[5] = jnp.where(z_down, ns[5], 0.0)
                    ws = [scale3 * (k + n) for n in ns]
                    total = (ws[0] + ws[1]) + (ws[2] + ws[3]) + (ws[4] + ws[5])
                    ok = k > 0.0
                    inv = jnp.where(ok, OMEGA / jnp.where(ok, total, 1.0), 0.0)
                    ws[4] = jnp.where(z_up, ws[4], 0.0)
                    ws[5] = jnp.where(z_down, ws[5], 0.0)
                    for j, w in enumerate(ws):
                        r["W"][6 * (2 * b + a) + j] = inv * w
        start = [[got(2 * b + a) for a in (0, 1)] for b in (0, 1)]

        def coarse(_, flat):
            c = [[flat[0], flat[1]], [flat[2], flat[3]]]
            new = []
            for b in (0, 1):
                for a in (0, 1):
                    t = [r["W"][6 * (2 * b + a) + j] * n for j, n in enumerate(sides(c, b, a))]
                    v = start[b][a] + (1.0 - OMEGA) * c[b][a]
                    new.append((v + (t[0] + t[1])) + ((t[2] + t[3]) + (t[4] + t[5])))
            return tuple(new)

        flat = (start[0][0], start[0][1], start[1][0], start[1][1])
        flat = lax.fori_loop(0, SWEEPS - 1, coarse, flat)

        ring = r["VF2"].at[cyc]
        remote(ring.at[0:6], ring.at[0:6], S_SEM + cyc, 1, 0).wait_recv()
        cell = row // 2
        want = (lane & ~7) + (R - 1) + (cell + 1) // 2
        full2 = {}
        for i in range(8):
            v = ring[i]
            if 2 <= i < 6:
                v = jnp.where((row >= 2) & (row < 6), v2[i], v)
            full2[i] = jnp.where(r["K2"][i] > 0.0, v, 0.0)
        for i in range(4):
            s, a = R - 1 + (i + 1) // 2, (i + 1) % 2
            e0 = jnp.broadcast_to(flat[a][s : s + 1], (8, 128))
            e1 = jnp.broadcast_to(flat[2 + a][s : s + 1], (8, 128))
            e = jnp.take_along_axis(jnp.where(cell % 2 == 0, e1, e0), want, axis=1)
            r["VE2"][2 * i] = full2[2 * i] + e
            r["VE2"][2 * i + 1] = full2[2 * i + 1] + e

        up2 = {}
        for i in range(1, 7):
            v, n = around(2, r["VE2"], i)
            up2[i] = (1.0 - OMEGA) * v + full2[i] + r["I2"][i] * n
        for i in range(1, 7):
            r["S2"][i, pl.ds(0, 8, 2), :] = up2[i]
            r["S2"][i, pl.ds(1, 8, 2), :] = up2[i]

        unrolled(2, 14, lambda i: [(r["VE1"], i, r["V1"][i] + r["S2"][i // 2])])

        def up1(j, _):
            new = []
            for q in range(5):
                i = 3 + 5 * j + q
                v, n = around(1, r["VE1"], i)
                new.append((i, (1.0 - OMEGA) * v + r["V1"][i] + r["I1"][i] * n))
            for i, v in new:
                r["F1"][i, pl.ds(0, 16, 2), :] = v
                r["F1"][i, pl.ds(1, 16, 2), :] = v
            return 0

        lax.fori_loop(0, 2, up1, 0)

        def add0(i):
            e = r["F1"][i]
            return [(r["VE"], 2 * i + q, r["V"][2 * i + q] + e) for q in (0, 1)]

        planes(3, 13, 5, add0)

        def up0(i, c=cyc):
            v, n = around(0, r["VE"], i)
            if c == 0:
                v = (1.0 - OMEGA) * v + r["V"][i] + r["I0"][i] * n
            else:
                v = (1.0 - OMEGA) * v + r["I0"][i] * (r["G"][i] + n)
            v = v[8:24]
            if c == CYCLES - 1:
                return [(out, i - 8, v)]
            return [(r["VB"].at[:, 8:24], i, v), (r["F0"], i - 8, v)]

        planes(8, 24, 4, up0)
        if cyc < CYCLES - 1:
            send_field()

    for name in SEM:
        y_faces(name).wait_send()
        the_rest(name).wait_send()
    field().wait_send()
    for cyc in range(CYCLES):
        ring = r["VF2"].at[cyc, 0:6]
        remote(ring, ring, S_SEM + cyc, 1, 0).wait_send()
        rows = r["C"].at[cyc, 0 : len(PARTNERS)]
        remote(rows, rows, C_SEM + cyc, 1, 0).wait_send()


SEM = {"M": 0, "G": 2}
V_SEM, S_SEM, C_SEM = 4, 5, 5 + CYCLES
CUT = {"M": 8, "G": 6, "VB": 7}
FILL = {"M": "FM", "G": "FZ"}
SPARE = {"M": "MS", "G": "GS"}
FOUR = ((1, 0), (-1, 0), (0, 1), (0, -1))


def scratch():
    f = jnp.float32

    def vm(*shape):
        return pltpu.VMEM(shape, f)

    a, b, c = vm(32, 32, 128), vm(16, 16, 128), vm(8, 8, 128)
    dma = pltpu.SemaphoreType.DMA
    shapes = [a, pltpu.VMEM((32, 32, 128), jnp.int32)] + [a] * 9
    shapes += [vm(16, 32, 128)] * 2 + [b] * 8 + [vm(8, 16, 128)] * 2
    shapes += [c] + [vm(CYCLES, 8, 8, 128)] * 2 + [c] * 5 + [vm(4, 8, 128), b]
    shapes += [vm(CYCLES, 64, 128), vm(24, 8, 128)]
    sems = C_SEM + CYCLES
    i16, i32 = (pltpu.VMEM((n, n, 128), jnp.int32) for n in (16, 32))
    shapes += [i16, b, i32, a, a]
    return shapes + [dma((2,)), dma((sems,)), dma((sems,)), pltpu.SemaphoreType.REGULAR((3,))]


def local(right_side, material, conductivity):
    nx, ny = lax.axis_size("gx"), lax.axis_size("gy")
    return pl.pallas_call(
        functools.partial(kernel, nx, ny),
        out_shape=jax.ShapeDtypeStruct(right_side.shape, right_side.dtype),
        in_specs=[
            pl.BlockSpec(memory_space=pltpu.SMEM),
            pl.BlockSpec(memory_space=pl.ANY),
            pl.BlockSpec(memory_space=pl.ANY),
        ],
        out_specs=pl.BlockSpec(memory_space=pltpu.VMEM),
        scratch_shapes=scratch(),
        compiler_params=pltpu.CompilerParams(collective_id=0, has_side_effects=True),
        name="vcycles",
    )(conductivity, right_side, material)


def solution(mesh):
    return jax.shard_map(
        local,
        mesh=mesh,
        in_specs=(P("gx", "gy", None), P("gx", "gy", None), P()),
        out_specs=P("gx", "gy", None),
        check_vma=False,
    )
```

```python
import functools

import jax
import jax.numpy as jnp
from jax import lax
from jax.experimental import pallas as pl
from jax.experimental.pallas import tpu as pltpu
from jax.sharding import PartitionSpec as P

MESH = pl.DeviceIdType.MESH
CYCLES = 2
SWEEPS = 6
OMEGA = 0.8
NMAT = 16
H = 8
R = 3
DIRS = tuple((a, b) for a in (-1, 0, 1) for b in (-1, 0, 1) if (a, b) != (0, 0))


STEPS = tuple(range(-R, R + 1))
PARTNERS = tuple(
    sorted(
        ((a, b) for a in STEPS for b in STEPS if (a or b) and abs(a) + abs(b) <= R + 1),
        key=lambda d: -abs(d[0]) - 1.25 * abs(d[1]),
    )
)


def send_part(s, n=H):
    return {1: slice(16 - n, 16), -1: slice(0, n), 0: slice(0, 16)}[s]


def halo_part(s, n=H):
    return {1: slice(24, 24 + n), -1: slice(8 - n, 8), 0: slice(8, 24)}[s]


def roll(v, shift, axis):
    return pltpu.roll(v, shift % v.shape[axis], axis)


def iota(shape, axis):
    return lax.broadcasted_iota(jnp.int32, shape, axis)


def pair_swap(v, apart, axis):
    low = (iota(v.shape, axis) & apart) == 0
    return jnp.where(low, roll(v, -apart, axis), roll(v, apart, axis))


def kernel(nx, ny, cond, g_hbm, m_hbm, out, *refs):
    names = (
        "G", "M", "K0", "V", "VB", "VE", "I0", "T0", "X0", "Y0", "Z0", "S0", "F1",
        "K1", "V1", "G1", "VE1", "I1", "X1", "Y1", "Z1", "S1", "S2",
        "K2", "V2", "VF2", "VE2", "I2", "X2", "Y2", "Z2", "K3", "F0", "C", "W",
        "FM", "FZ", "MS", "GS", "VS", "lsem", "send", "recv", "ready",
    )
    r = dict(zip(names, refs, strict=True))
    px, py = lax.axis_index("gx"), lax.axis_index("gy")
    x_ok = {d: (px + d >= 0) & (px + d < nx) for d in STEPS}
    y_ok = {d: (py + d >= 0) & (py + d < ny) for d in STEPS}

    xs = {d: lax.rem(px + (d + nx), nx) if d else px for d in STEPS}
    ys = {d: lax.rem(py + (d + ny), ny) if d else py for d in STEPS}

    def exists(a, b):
        if a == 0:
            return y_ok[b]
        return x_ok[a] if b == 0 else x_ok[a] & y_ok[b]

    def remote(src, dst, sem, a, b):
        return pltpu.make_async_remote_copy(
            src_ref=src, dst_ref=dst, send_sem=r["send"].at[sem], recv_sem=r["recv"].at[sem],
            device_id=(xs[a], ys[b]), device_id_type=MESH,
        )

    def push(src, dst, sem, a, b, hole, fill, spare):
        ok = exists(a, b)
        pl.when(ok)(lambda: remote(src, dst, sem, a, b).start())

        @pl.when(jnp.logical_not(ok))
        def _():
            pltpu.make_async_copy(fill, hole, r["recv"].at[sem]).start()
            pltpu.make_async_copy(fill, spare, r["send"].at[sem]).start()

    def tell(sem):
        for a, b in FOUR:
            pl.semaphore_signal(sem, inc=1, device_id=(xs[a], ys[b]), device_id_type=MESH)

    own = (slice(8, 24), slice(8, 24))
    lg = pltpu.make_async_copy(g_hbm, r["G"].at[own], r["lsem"].at[0])
    lm = pltpu.make_async_copy(m_hbm, r["M"].at[own], r["lsem"].at[1])
    lm.start()
    lg.start()
    barrier = pltpu.get_barrier_semaphore()
    tell(barrier)
    r["FM"][...] = jnp.full((16, 16, 128), NMAT, jnp.int32)
    r["FZ"][...] = jnp.zeros((16, 16, 128), jnp.float32)
    lane = iota((8, 128), 1)
    row = iota((8, 128), 0)
    slot = lane & 7
    table = jnp.zeros((8, 128), jnp.float32)
    for i in range(NMAT):
        table = jnp.where(lane == i, cond[i], table)
    table32 = jnp.concatenate([table] * 4, 0)
    pl.semaphore_wait(barrier, 4)
    tell(r["ready"].at[0])

    def send_faces(src, name, along_y):
        dst, fill, spare, sem = r[name], r[FILL[name]], r[SPARE[name]], SEM[name]
        for q in (1, -1):
            a, b = (0, q) if along_y else (q, 0)
            hole = (halo_part(a), halo_part(b))
            push(
                src.at[send_part(a), send_part(b)], dst.at[halo_part(-a), halo_part(-b)],
                sem if along_y else sem + 1, a, b,
                dst.at[hole], fill.at[0 : 8 if a else 16, 0 : 8 if b else 16], spare.at[hole],
            )

    def send_corners(name):
        dst, fill, spare, n = r[name], r[FILL[name]], r[SPARE[name]], CUT[name]
        for a in (1, -1):
            near_planes = slice(24 - n, 24) if a == 1 else slice(8, 8 + n)
            for b in (1, -1):
                hole = (halo_part(a, n), halo_part(b))
                push(
                    dst.at[near_planes, halo_part(b)], dst.at[halo_part(-a, n), halo_part(b)],
                    SEM[name] + 1, a, 0, dst.at[hole], fill.at[0:n, 0:8], spare.at[hole],
                )

    def send_field():
        dst, n = r["VB"], CUT["VB"]
        for a, b in sorted(DIRS, key=lambda d: -abs(d[0]) - abs(d[1])):
            m = n if a and b else H
            hole = (halo_part(a, m), halo_part(b))
            tall, wide = m if a else 16, 8 if b else 16
            push(
                r["F0"].at[send_part(a, m), send_part(b)],
                dst.at[halo_part(-a, m), halo_part(-b)], V_SEM, a, b,
                dst.at[hole], r["FZ"].at[0:tall, 0:wide], r["VS"].at[hole],
            )

    def field():
        view = r["VB"].at[0 : 16 + CUT["VB"]]
        return remote(view, view, V_SEM, 1, 0)

    def y_faces(name):
        view = r[name].at[0:8]
        return remote(view, view, SEM[name], 1, 0)

    def the_rest(name):
        view = r[name].at[0 : 8 + CUT[name]]
        return remote(view, view, SEM[name] + 1, 1, 0)

    send_faces(m_hbm, "M", True)
    send_faces(m_hbm, "M", False)
    send_faces(g_hbm, "G", True)
    y_faces("M").wait_recv()
    send_corners("M")
    send_faces(g_hbm, "G", False)
    pl.semaphore_wait(r["ready"].at[0], 4)
    tell(r["ready"].at[1])
    lm.wait()

    def planes(lo, hi, step, one):
        def body(j, _):
            done = []
            for q in range(step):
                done += one(lo + j * step + q)
            for ref, i, v in done:
                ref[i] = v
            return 0

        lax.fori_loop(0, (hi - lo) // step, body, 0)

    def unrolled(lo, hi, one):
        done = []
        for i in range(lo, hi):
            done += one(i)
        for ref, i, v in done:
            ref[i] = v

    def face_values(lv, i):
        scale = 0.5 * 0.25**lv
        step = 1 << lv
        k_ref = r[f"K{lv}"]
        k, kn = k_ref[i], k_ref[i + 1]
        ln = iota(k.shape, 1)
        below, above = ln < 128 - step, ln >= step
        ky = roll(k, -1, 0)
        kz = roll(k, -step, 1)
        s = 6.0 * k + (kn + k_ref[i - 1]) + (ky + roll(k, 1, 0))
        s = s + jnp.where(below, kz, 0.0) + jnp.where(above, roll(k, step, 1), 0.0)
        total = scale * s
        inside = k > 0.0
        inv = jnp.where(inside, OMEGA / total, 0.0)
        res = [
            (r[f"X{lv}"], i, scale * (k + kn)),
            (r[f"Y{lv}"], i, scale * (k + ky)),
            (r[f"Z{lv}"], i, jnp.where(below, scale * (k + kz), 0.0)),
            (r[f"I{lv}"], i, inv),
        ]
        if lv == 0:
            res.append((r["T0"], i, total))
        return res

    def around(lv, v_ref, i):
        step = 1 << lv
        v = v_ref[i]
        x, y, z = r[f"X{lv}"], r[f"Y{lv}"][i], r[f"Z{lv}"][i]
        n = x[i] * v_ref[i + 1] + x[i - 1] * v_ref[i - 1]
        n = n + (y * roll(v, -1, 0) + roll(y * v, 1, 0))
        return v, n + (z * roll(v, -step, 1) + roll(z * v, step, 1))

    def z_mean(s, lv):
        return 0.125 * (s + pair_swap(s, 1 << lv, 1))

    def y_pairs(ref, i, n):
        return ref[i, pl.ds(0, n, 2), :] + ref[i, pl.ds(1, n, 2), :]

    def to_three(t):
        return z_mean(t + pair_swap(t, 1, 0), 2)

    def look(i):
        k = [jnp.take_along_axis(table32, r["M"][2 * i + q], axis=1) for q in (0, 1)]
        return [(r["K0"], 2 * i, k[0]), (r["K0"], 2 * i + 1, k[1]), (r["S0"], i, k[0] + k[1])]

    def mean1(i):
        return [(r["K1"], i, z_mean(y_pairs(r["S0"], i, 16), 0))]

    faces0 = functools.partial(face_values, 0)
    planes(4, 12, 4, look)
    y_faces("G").wait_recv()
    send_corners("G")
    planes(4, 12, 8, mean1)
    planes(9, 23, 2, faces0)
    the_rest("M").wait_recv()
    pl.semaphore_wait(r["ready"].at[1], 4)
    tell(r["ready"].at[2])
    planes(0, 4, 4, look)
    planes(12, 16, 4, look)
    planes(0, 4, 4, mean1)
    planes(12, 16, 4, mean1)
    unrolled(0, 8, lambda i: [(r["S1"], i, r["K1"][2 * i] + r["K1"][2 * i + 1])])
    unrolled(0, 8, lambda i: [(r["K2"], i, z_mean(y_pairs(r["S1"], i, 8), 1))])
    unrolled(0, 4, lambda i: [(r["K3"], i, to_three(r["K2"][2 * i] + r["K2"][2 * i + 1]))])
    for lv, scale in ((0, 0.5), (1, 0.125), (2, 0.03125)):
        r[f"X{lv}"][0] = scale * (r[f"K{lv}"][0] + r[f"K{lv}"][1])
    planes(1, 9, 4, faces0)
    planes(23, 31, 4, faces0)
    planes(1, 15, 7, functools.partial(face_values, 1))
    unrolled(1, 7, functools.partial(face_values, 2))

    scale3 = 0.5 * 0.25**3
    z_up, z_down = lane < 120, lane >= 8
    inv3 = []
    for i in (1, 2):
        k = r["K3"][i]
        s = r["K3"][i - 1] + r["K3"][i + 1] + roll(k, 2, 0) + roll(k, -2, 0)
        s = s + jnp.where(z_up, roll(k, -8, 1), 0.0) + jnp.where(z_down, roll(k, 8, 1), 0.0)
        inv3.append(OMEGA / (scale3 * (6.0 * k + s)))

    lg.wait()
    the_rest("G").wait_recv()
    planes(1, 31, 6, lambda i: [(r["V"], i, r["I0"][i] * r["G"][i])])

    far_x, far_y = row - R, slot - R
    here = (px + far_x >= 0) & (px + far_x < nx) & (py + far_y >= 0) & (py + far_y < ny)
    here = here & (far_x <= R) & (jnp.abs(far_x) + jnp.abs(far_y) <= R + 1)

    def side_copy(a, b, cyc):
        out_part = {1: slice(4, 6), -1: slice(2, 4), 0: slice(2, 6)}
        in_part = {1: slice(6, 8), -1: slice(0, 2), 0: slice(2, 6)}
        return remote(
            r["V2"].at[cyc, out_part[a], out_part[b]],
            r["VF2"].at[cyc, in_part[-a], in_part[-b]],
            S_SEM + cyc, a, b,
        )

    def row_of(a, b):
        return 8 * (b + R) + a + R

    for cyc in range(CYCLES):
        if cyc:
            field().wait_recv()

            def sweep(i):
                v, n = around(0, r["VB"], i)
                return [(r["V"], i, (1.0 - OMEGA) * v + r["I0"][i] * (r["G"][i] + n))]

            planes(1, 31, 3, sweep)

        def resid0(i, first=cyc == 0):
            v, n = around(0, r["V"], i)
            if first:
                return (1.0 - OMEGA) * r["G"][i] + n
            return r["G"][i] - r["T0"][i] * v + n

        planes(1, 15, 2, lambda i: [(r["S0"], i, resid0(2 * i) + resid0(2 * i + 1))])

        def start1(i):
            g = z_mean(y_pairs(r["S0"], i, 16), 0)
            return [(r["G1"], i, g), (r["V1"], i, r["I1"][i] * g)]

        planes(1, 15, 7, start1)

        def resid1(i):
            _, n = around(1, r["V1"], i)
            return (1.0 - OMEGA) * r["G1"][i] + n

        planes(1, 7, 3, lambda i: [(r["S1"], i, resid1(2 * i) + resid1(2 * i + 1))])
        v2 = r["V2"].at[cyc]
        g2 = {i: z_mean(y_pairs(r["S1"], i, 8), 1) for i in range(1, 7)}
        unrolled(1, 7, lambda i: [(v2, i, r["I2"][i] * g2[i])])

        def resid2(i):
            _, n = around(2, v2, i)
            return (1.0 - OMEGA) * g2[i] + n

        first3 = []
        for a in (0, 1):
            first3.append(inv3[a] * to_three(resid2(2 * a + 2) + resid2(2 * a + 3)))
        mine = jnp.zeros((8, 128), jnp.float32)
        for f, pair in ((0, first3), (1, [r["K3"][1], r["K3"][2]])):
            for a in (0, 1):
                for b in (0, 1):
                    mine = jnp.where(slot == 4 * f + 2 * b + a, roll(pair[a], -2 - 2 * b, 0), mine)
        near = r["C"].at[cyc]
        near[row_of(0, 0) : row_of(0, 0) + 1] = mine[0:1]
        if cyc == 0:
            pl.semaphore_wait(r["ready"].at[2], 4)
        for a, b in DIRS:
            side_copy(a, b, cyc).start()
        my_row = near.at[row_of(0, 0) : row_of(0, 0) + 1]
        for a, b in PARTNERS:
            there = row_of(-a, -b)
            remote(my_row, near.at[there : there + 1], C_SEM + cyc, a, b).start()

        rows = near.at[0 : len(PARTNERS)]
        remote(rows, rows, C_SEM + cyc, 1, 0).wait_recv()

        tiles = [near[8 * s : 8 * s + 8] for s in range(2 * R + 1)]

        def got(p):
            v = jnp.zeros((8, 128), jnp.float32)
            for s, t in enumerate(tiles):
                v = jnp.where(here & (slot == s), roll(t, s - p, 1), v)
            return v

        def sides(c, b, a):
            xp = c[b][1] if a == 0 else roll(c[b][0], -1, 0)
            xm = c[b][0] if a == 1 else roll(c[b][1], 1, 0)
            yp = c[1][a] if b == 0 else roll(c[0][a], -1, 1)
            ym = c[0][a] if b == 1 else roll(c[1][a], 1, 1)
            return xp, xm, yp, ym, roll(c[b][a], -8, 1), roll(c[b][a], 8, 1)

        if cyc == 0:
            k3 = [[got(4 + 2 * b + a) for a in (0, 1)] for b in (0, 1)]
            for b in (0, 1):
                for a in (0, 1):
                    k = k3[b][a]
                    ns = list(sides(k3, b, a))
                    ns[4] = jnp.where(z_up, ns[4], 0.0)
                    ns[5] = jnp.where(z_down, ns[5], 0.0)
                    ws = [scale3 * (k + n) for n in ns]
                    total = (ws[0] + ws[1]) + (ws[2] + ws[3]) + (ws[4] + ws[5])
                    ok = k > 0.0
                    inv = jnp.where(ok, OMEGA / jnp.where(ok, total, 1.0), 0.0)
                    ws[4] = jnp.where(z_up, ws[4], 0.0)
                    ws[5] = jnp.where(z_down, ws[5], 0.0)
                    for j, w in enumerate(ws):
                        r["W"][6 * (2 * b + a) + j] = inv * w
        start = [[got(2 * b + a) for a in (0, 1)] for b in (0, 1)]

        def coarse(_, flat):
            c = [[flat[0], flat[1]], [flat[2], flat[3]]]
            new = []
            for b in (0, 1):
                for a in (0, 1):
                    t = [r["W"][6 * (2 * b + a) + j] * n for j, n in enumerate(sides(c, b, a))]
                    v = start[b][a] + (1.0 - OMEGA) * c[b][a]
                    new.append((v + (t[0] + t[1])) + ((t[2] + t[3]) + (t[4] + t[5])))
            return tuple(new)

        flat = (start[0][0], start[0][1], start[1][0], start[1][1])
        flat = lax.fori_loop(0, SWEEPS - 1, coarse, flat)

        ring = r["VF2"].at[cyc]
        remote(ring.at[0:6], ring.at[0:6], S_SEM + cyc, 1, 0).wait_recv()
        cell = row // 2
        want = (lane & ~7) + (R - 1) + (cell + 1) // 2
        full2 = {}
        for i in range(8):
            v = ring[i]
            if 2 <= i < 6:
                v = jnp.where((row >= 2) & (row < 6), v2[i], v)
            full2[i] = jnp.where(r["K2"][i] > 0.0, v, 0.0)
        for i in range(4):
            s, a = R - 1 + (i + 1) // 2, (i + 1) % 2
            e0 = jnp.broadcast_to(flat[a][s : s + 1], (8, 128))
            e1 = jnp.broadcast_to(flat[2 + a][s : s + 1], (8, 128))
            e = jnp.take_along_axis(jnp.where(cell % 2 == 0, e1, e0), want, axis=1)
            r["VE2"][2 * i] = full2[2 * i] + e
            r["VE2"][2 * i + 1] = full2[2 * i + 1] + e

        up2 = {}
        for i in range(1, 7):
            v, n = around(2, r["VE2"], i)
            up2[i] = (1.0 - OMEGA) * v + full2[i] + r["I2"][i] * n
        for i in range(1, 7):
            r["S2"][i, pl.ds(0, 8, 2), :] = up2[i]
            r["S2"][i, pl.ds(1, 8, 2), :] = up2[i]

        unrolled(2, 14, lambda i: [(r["VE1"], i, r["V1"][i] + r["S2"][i // 2])])

        def up1(j, _):
            new = []
            for q in range(5):
                i = 3 + 5 * j + q
                v, n = around(1, r["VE1"], i)
                new.append((i, (1.0 - OMEGA) * v + r["V1"][i] + r["I1"][i] * n))
            for i, v in new:
                r["F1"][i, pl.ds(0, 16, 2), :] = v
                r["F1"][i, pl.ds(1, 16, 2), :] = v
            return 0

        lax.fori_loop(0, 2, up1, 0)

        def add0(i):
            e = r["F1"][i]
            return [(r["VE"], 2 * i + q, r["V"][2 * i + q] + e) for q in (0, 1)]

        planes(3, 13, 5, add0)

        def up0(i, c=cyc):
            v, n = around(0, r["VE"], i)
            if c == 0:
                v = (1.0 - OMEGA) * v + r["V"][i] + r["I0"][i] * n
            else:
                v = (1.0 - OMEGA) * v + r["I0"][i] * (r["G"][i] + n)
            v = v[8:24]
            if c == CYCLES - 1:
                return [(out, i - 8, v)]
            return [(r["VB"].at[:, 8:24], i, v), (r["F0"], i - 8, v)]

        planes(8, 24, 4, up0)
        if cyc < CYCLES - 1:
            send_field()

    for name in SEM:
        y_faces(name).wait_send()
        the_rest(name).wait_send()
    field().wait_send()
    for cyc in range(CYCLES):
        ring = r["VF2"].at[cyc, 0:6]
        remote(ring, ring, S_SEM + cyc, 1, 0).wait_send()
        rows = r["C"].at[cyc, 0 : len(PARTNERS)]
        remote(rows, rows, C_SEM + cyc, 1, 0).wait_send()


SEM = {"M": 0, "G": 2}
V_SEM, S_SEM, C_SEM = 4, 5, 5 + CYCLES
CUT = {"M": 8, "G": 6, "VB": 7}
FILL = {"M": "FM", "G": "FZ"}
SPARE = {"M": "MS", "G": "GS"}
FOUR = ((1, 0), (-1, 0), (0, 1), (0, -1))


def scratch():
    f = jnp.float32

    def vm(*shape):
        return pltpu.VMEM(shape, f)

    a, b, c = vm(32, 32, 128), vm(16, 16, 128), vm(8, 8, 128)
    dma = pltpu.SemaphoreType.DMA
    shapes = [a, pltpu.VMEM((32, 32, 128), jnp.int32)] + [a] * 9
    shapes += [vm(16, 32, 128)] * 2 + [b] * 8 + [vm(8, 16, 128)] * 2
    shapes += [c] + [vm(CYCLES, 8, 8, 128)] * 2 + [c] * 5 + [vm(4, 8, 128), b]
    shapes += [vm(CYCLES, 64, 128), vm(24, 8, 128)]
    sems = C_SEM + CYCLES
    i16, i32 = (pltpu.VMEM((n, n, 128), jnp.int32) for n in (16, 32))
    shapes += [i16, b, i32, a, a]
    return shapes + [dma((2,)), dma((sems,)), dma((sems,)), pltpu.SemaphoreType.REGULAR((3,))]


def local(right_side, material, conductivity):
    nx, ny = lax.axis_size("gx"), lax.axis_size("gy")
    return pl.pallas_call(
        functools.partial(kernel, nx, ny),
        out_shape=pltpu.VMEM(right_side.shape, right_side.dtype),
        in_specs=[
            pl.BlockSpec(memory_space=pltpu.SMEM),
            pl.BlockSpec(memory_space=pl.ANY),
            pl.BlockSpec(memory_space=pl.ANY),
        ],
        out_specs=pl.BlockSpec(memory_space=pltpu.VMEM),
        scratch_shapes=scratch(),
        compiler_params=pltpu.CompilerParams(collective_id=0, has_side_effects=True),
        name="vcycles",
    )(conductivity, right_side, material)


def solution(mesh):
    return jax.shard_map(
        local,
        mesh=mesh,
        in_specs=(P("gx", "gy", None), P("gx", "gy", None), P()),
        out_specs=P("gx", "gy", None),
        check_vma=False,
    )
```

```python
import functools

import jax
import jax.numpy as jnp
from jax import lax
from jax.experimental import pallas as pl
from jax.experimental.pallas import tpu as pltpu
from jax.sharding import PartitionSpec as P

MESH = pl.DeviceIdType.MESH
CYCLES = 2
SWEEPS = 6
OMEGA = 0.8
NMAT = 16
H = 8
R = 3
DIRS = tuple((a, b) for a in (-1, 0, 1) for b in (-1, 0, 1) if (a, b) != (0, 0))


STEPS = tuple(range(-R, R + 1))
PARTNERS = tuple(
    sorted(
        ((a, b) for a in STEPS for b in STEPS if (a or b) and abs(a) + abs(b) <= R + 1),
        key=lambda d: -abs(d[0]) - 1.25 * abs(d[1]),
    )
)


def send_part(s, n=H):
    return {1: slice(16 - n, 16), -1: slice(0, n), 0: slice(0, 16)}[s]


def halo_part(s, n=H):
    return {1: slice(24, 24 + n), -1: slice(8 - n, 8), 0: slice(8, 24)}[s]


def roll(v, shift, axis):
    return pltpu.roll(v, shift % v.shape[axis], axis)


def iota(shape, axis):
    return lax.broadcasted_iota(jnp.int32, shape, axis)


def pair_swap(v, apart, axis):
    low = (iota(v.shape, axis) & apart) == 0
    return jnp.where(low, roll(v, -apart, axis), roll(v, apart, axis))


def kernel(nx, ny, cond, g_hbm, m_hbm, out, *refs):
    names = (
        "G", "M", "K0", "V", "VB", "VE", "I0", "T0", "X0", "Y0", "Z0", "S0", "F1",
        "K1", "V1", "G1", "VE1", "I1", "X1", "Y1", "Z1", "S1", "S2",
        "K2", "V2", "VF2", "VE2", "I2", "X2", "Y2", "Z2", "K3", "F0", "C", "W",
        "FM", "FZ", "MS", "GS", "VS", "lsem", "send", "recv", "ready",
    )
    r = dict(zip(names, refs, strict=True))
    px, py = lax.axis_index("gx"), lax.axis_index("gy")
    x_ok = {d: (px + d >= 0) & (px + d < nx) for d in STEPS}
    y_ok = {d: (py + d >= 0) & (py + d < ny) for d in STEPS}

    xs = {d: lax.rem(px + (d + nx), nx) if d else px for d in STEPS}
    ys = {d: lax.rem(py + (d + ny), ny) if d else py for d in STEPS}

    def exists(a, b):
        if a == 0:
            return y_ok[b]
        return x_ok[a] if b == 0 else x_ok[a] & y_ok[b]

    def remote(src, dst, sem, a, b):
        return pltpu.make_async_remote_copy(
            src_ref=src, dst_ref=dst, send_sem=r["send"].at[sem], recv_sem=r["recv"].at[sem],
            device_id=(xs[a], ys[b]), device_id_type=MESH,
        )

    def push(src, dst, sem, a, b, hole, fill, spare):
        ok = exists(a, b)
        pl.when(ok)(lambda: remote(src, dst, sem, a, b).start())

        @pl.when(jnp.logical_not(ok))
        def _():
            pltpu.make_async_copy(fill, hole, r["recv"].at[sem]).start()
            pltpu.make_async_copy(fill, spare, r["send"].at[sem]).start()

    def tell(sem):
        for a, b in FOUR:
            pl.semaphore_signal(sem, inc=1, device_id=(xs[a], ys[b]), device_id_type=MESH)

    own = (slice(8, 24), slice(8, 24))
    lg = pltpu.make_async_copy(g_hbm, r["G"].at[own], r["lsem"].at[0])
    lm = pltpu.make_async_copy(m_hbm, r["M"].at[own], r["lsem"].at[1])
    lm.start()
    lg.start()
    barrier = pltpu.get_barrier_semaphore()
    tell(barrier)
    r["FM"][...] = jnp.full((16, 16, 128), NMAT, jnp.int32)
    r["FZ"][...] = jnp.zeros((16, 16, 128), jnp.float32)
    lane = iota((8, 128), 1)
    row = iota((8, 128), 0)
    slot = lane & 7
    table = jnp.zeros((8, 128), jnp.float32)
    for i in range(NMAT):
        table = jnp.where(lane == i, cond[i], table)
    table32 = jnp.concatenate([table] * 4, 0)
    pl.semaphore_wait(barrier, 4)
    tell(r["ready"].at[0])

    def send_faces(src, name, along_y):
        dst, fill, spare, sem = r[name], r[FILL[name]], r[SPARE[name]], SEM[name]
        for q in (1, -1):
            a, b = (0, q) if along_y else (q, 0)
            hole = (halo_part(a), halo_part(b))
            push(
                src.at[send_part(a), send_part(b)], dst.at[halo_part(-a), halo_part(-b)],
                sem if along_y else sem + 1, a, b,
                dst.at[hole], fill.at[0 : 8 if a else 16, 0 : 8 if b else 16], spare.at[hole],
            )

    def send_corners(name):
        dst, fill, spare, n = r[name], r[FILL[name]], r[SPARE[name]], CUT[name]
        for a in (1, -1):
            near_planes = slice(24 - n, 24) if a == 1 else slice(8, 8 + n)
            for b in (1, -1):
                hole = (halo_part(a, n), halo_part(b))
                push(
                    dst.at[near_planes, halo_part(b)], dst.at[halo_part(-a, n), halo_part(b)],
                    SEM[name] + 1, a, 0, dst.at[hole], fill.at[0:n, 0:8], spare.at[hole],
                )

    def send_field():
        dst, n = r["VB"], CUT["VB"]
        for a, b in sorted(DIRS, key=lambda d: (abs(d[0]), -abs(d[1]))):
            m = n if a and b else H
            hole = (halo_part(a, m), halo_part(b))
            tall, wide = m if a else 16, 8 if b else 16
            push(
                r["F0"].at[send_part(a, m), send_part(b)],
                dst.at[halo_part(-a, m), halo_part(-b)], V_SEM + abs(a), a, b,
                dst.at[hole], r["FZ"].at[0:tall, 0:wide], r["VS"].at[hole],
            )

    def field(rest):
        view = r["VB"].at[0 : 8 + CUT["VB"] if rest else 8]
        return remote(view, view, V_SEM + rest, 1, 0)

    def y_faces(name):
        view = r[name].at[0:8]
        return remote(view, view, SEM[name], 1, 0)

    def the_rest(name):
        view = r[name].at[0 : 8 + CUT[name]]
        return remote(view, view, SEM[name] + 1, 1, 0)

    send_faces(m_hbm, "M", True)
    send_faces(m_hbm, "M", False)
    send_faces(g_hbm, "G", True)
    y_faces("M").wait_recv()
    send_corners("M")
    send_faces(g_hbm, "G", False)
    pl.semaphore_wait(r["ready"].at[0], 4)
    tell(r["ready"].at[1])
    lm.wait()

    def planes(lo, hi, step, one):
        def body(j, _):
            done = []
            for q in range(step):
                done += one(lo + j * step + q)
            for ref, i, v in done:
                ref[i] = v
            return 0

        lax.fori_loop(0, (hi - lo) // step, body, 0)

    def unrolled(lo, hi, one):
        done = []
        for i in range(lo, hi):
            done += one(i)
        for ref, i, v in done:
            ref[i] = v

    def face_values(lv, i):
        scale = 0.5 * 0.25**lv
        step = 1 << lv
        k_ref = r[f"K{lv}"]
        k, kn = k_ref[i], k_ref[i + 1]
        ln = iota(k.shape, 1)
        below, above = ln < 128 - step, ln >= step
        ky = roll(k, -1, 0)
        kz = roll(k, -step, 1)
        s = 6.0 * k + (kn + k_ref[i - 1]) + (ky + roll(k, 1, 0))
        s = s + jnp.where(below, kz, 0.0) + jnp.where(above, roll(k, step, 1), 0.0)
        total = scale * s
        inside = k > 0.0
        inv = jnp.where(inside, OMEGA / total, 0.0)
        res = [
            (r[f"X{lv}"], i, scale * (k + kn)),
            (r[f"Y{lv}"], i, scale * (k + ky)),
            (r[f"Z{lv}"], i, jnp.where(below, scale * (k + kz), 0.0)),
            (r[f"I{lv}"], i, inv),
        ]
        if lv == 0:
            res.append((r["T0"], i, total))
        return res

    def around(lv, v_ref, i):
        step = 1 << lv
        v = v_ref[i]
        x, y, z = r[f"X{lv}"], r[f"Y{lv}"][i], r[f"Z{lv}"][i]
        n = x[i] * v_ref[i + 1] + x[i - 1] * v_ref[i - 1]
        n = n + (y * roll(v, -1, 0) + roll(y * v, 1, 0))
        return v, n + (z * roll(v, -step, 1) + roll(z * v, step, 1))

    def z_mean(s, lv):
        return 0.125 * (s + pair_swap(s, 1 << lv, 1))

    def y_pairs(ref, i, n):
        return ref[i, pl.ds(0, n, 2), :] + ref[i, pl.ds(1, n, 2), :]

    def to_three(t):
        return z_mean(t + pair_swap(t, 1, 0), 2)

    def look(i):
        k = [jnp.take_along_axis(table32, r["M"][2 * i + q], axis=1) for q in (0, 1)]
        return [(r["K0"], 2 * i, k[0]), (r["K0"], 2 * i + 1, k[1]), (r["S0"], i, k[0] + k[1])]

    def mean1(i):
        return [(r["K1"], i, z_mean(y_pairs(r["S0"], i, 16), 0))]

    faces0 = functools.partial(face_values, 0)
    planes(4, 12, 4, look)
    y_faces("G").wait_recv()
    send_corners("G")
    planes(4, 12, 8, mean1)
    planes(9, 23, 2, faces0)
    the_rest("M").wait_recv()
    pl.semaphore_wait(r["ready"].at[1], 4)
    tell(r["ready"].at[2])
    planes(0, 4, 4, look)
    planes(12, 16, 4, look)
    planes(0, 4, 4, mean1)
    planes(12, 16, 4, mean1)
    unrolled(0, 8, lambda i: [(r["S1"], i, r["K1"][2 * i] + r["K1"][2 * i + 1])])
    unrolled(0, 8, lambda i: [(r["K2"], i, z_mean(y_pairs(r["S1"], i, 8), 1))])
    unrolled(0, 4, lambda i: [(r["K3"], i, to_three(r["K2"][2 * i] + r["K2"][2 * i + 1]))])
    for lv, scale in ((0, 0.5), (1, 0.125), (2, 0.03125)):
        r[f"X{lv}"][0] = scale * (r[f"K{lv}"][0] + r[f"K{lv}"][1])
    planes(1, 9, 4, faces0)
    planes(23, 31, 4, faces0)
    planes(1, 15, 7, functools.partial(face_values, 1))
    unrolled(1, 7, functools.partial(face_values, 2))

    scale3 = 0.5 * 0.25**3
    z_up, z_down = lane < 120, lane >= 8
    inv3 = []
    for i in (1, 2):
        k = r["K3"][i]
        s = r["K3"][i - 1] + r["K3"][i + 1] + roll(k, 2, 0) + roll(k, -2, 0)
        s = s + jnp.where(z_up, roll(k, -8, 1), 0.0) + jnp.where(z_down, roll(k, 8, 1), 0.0)
        inv3.append(OMEGA / (scale3 * (6.0 * k + s)))

    lg.wait()
    the_rest("G").wait_recv()
    planes(1, 31, 6, lambda i: [(r["V"], i, r["I0"][i] * r["G"][i])])

    far_x, far_y = row - R, slot - R
    here = (px + far_x >= 0) & (px + far_x < nx) & (py + far_y >= 0) & (py + far_y < ny)
    here = here & (far_x <= R) & (jnp.abs(far_x) + jnp.abs(far_y) <= R + 1)

    def side_copy(a, b, cyc):
        out_part = {1: slice(4, 6), -1: slice(2, 4), 0: slice(2, 6)}
        in_part = {1: slice(6, 8), -1: slice(0, 2), 0: slice(2, 6)}
        return remote(
            r["V2"].at[cyc, out_part[a], out_part[b]],
            r["VF2"].at[cyc, in_part[-a], in_part[-b]],
            S_SEM + cyc, a, b,
        )

    def row_of(a, b):
        return 8 * (b + R) + a + R

    for cyc in range(CYCLES):
        if cyc:

            def sweep(i):
                v, n = around(0, r["VB"], i)
                return [(r["V"], i, (1.0 - OMEGA) * v + r["I0"][i] * (r["G"][i] + n))]

            field(0).wait_recv()
            planes(9, 23, 2, sweep)

        def resid0(i, first=cyc == 0):
            v, n = around(0, r["V"], i)
            if first:
                return (1.0 - OMEGA) * r["G"][i] + n
            return r["G"][i] - r["T0"][i] * v + n

        def down0(i):
            return [(r["S0"], i, resid0(2 * i) + resid0(2 * i + 1))]

        if cyc:
            planes(5, 11, 2, down0)
            field(1).wait_recv()
            planes(1, 9, 4, sweep)
            planes(23, 31, 4, sweep)
            planes(1, 5, 2, down0)
            planes(11, 15, 2, down0)
        else:
            planes(1, 15, 2, down0)

        def start1(i):
            g = z_mean(y_pairs(r["S0"], i, 16), 0)
            return [(r["G1"], i, g), (r["V1"], i, r["I1"][i] * g)]

        planes(1, 15, 7, start1)

        def resid1(i):
            _, n = around(1, r["V1"], i)
            return (1.0 - OMEGA) * r["G1"][i] + n

        planes(1, 7, 3, lambda i: [(r["S1"], i, resid1(2 * i) + resid1(2 * i + 1))])
        v2 = r["V2"].at[cyc]
        g2 = {i: z_mean(y_pairs(r["S1"], i, 8), 1) for i in range(1, 7)}
        unrolled(1, 7, lambda i: [(v2, i, r["I2"][i] * g2[i])])

        def resid2(i):
            _, n = around(2, v2, i)
            return (1.0 - OMEGA) * g2[i] + n

        first3 = []
        for a in (0, 1):
            first3.append(inv3[a] * to_three(resid2(2 * a + 2) + resid2(2 * a + 3)))
        mine = jnp.zeros((8, 128), jnp.float32)
        for f, pair in ((0, first3), (1, [r["K3"][1], r["K3"][2]])):
            for a in (0, 1):
                for b in (0, 1):
                    mine = jnp.where(slot == 4 * f + 2 * b + a, roll(pair[a], -2 - 2 * b, 0), mine)
        near = r["C"].at[cyc]
        near[row_of(0, 0) : row_of(0, 0) + 1] = mine[0:1]
        if cyc == 0:
            pl.semaphore_wait(r["ready"].at[2], 4)
        for a, b in DIRS:
            side_copy(a, b, cyc).start()
        my_row = near.at[row_of(0, 0) : row_of(0, 0) + 1]
        for a, b in PARTNERS:
            there = row_of(-a, -b)
            remote(my_row, near.at[there : there + 1], C_SEM + cyc, a, b).start()

        rows = near.at[0 : len(PARTNERS)]
        remote(rows, rows, C_SEM + cyc, 1, 0).wait_recv()

        tiles = [near[8 * s : 8 * s + 8] for s in range(2 * R + 1)]

        def got(p):
            v = jnp.zeros((8, 128), jnp.float32)
            for s, t in enumerate(tiles):
                v = jnp.where(here & (slot == s), roll(t, s - p, 1), v)
            return v

        def sides(c, b, a):
            xp = c[b][1] if a == 0 else roll(c[b][0], -1, 0)
            xm = c[b][0] if a == 1 else roll(c[b][1], 1, 0)
            yp = c[1][a] if b == 0 else roll(c[0][a], -1, 1)
            ym = c[0][a] if b == 1 else roll(c[1][a], 1, 1)
            return xp, xm, yp, ym, roll(c[b][a], -8, 1), roll(c[b][a], 8, 1)

        if cyc == 0:
            k3 = [[got(4 + 2 * b + a) for a in (0, 1)] for b in (0, 1)]
            for b in (0, 1):
                for a in (0, 1):
                    k = k3[b][a]
                    ns = list(sides(k3, b, a))
                    ns[4] = jnp.where(z_up, ns[4], 0.0)
                    ns[5] = jnp.where(z_down, ns[5], 0.0)
                    ws = [scale3 * (k + n) for n in ns]
                    total = (ws[0] + ws[1]) + (ws[2] + ws[3]) + (ws[4] + ws[5])
                    ok = k > 0.0
                    inv = jnp.where(ok, OMEGA / jnp.where(ok, total, 1.0), 0.0)
                    ws[4] = jnp.where(z_up, ws[4], 0.0)
                    ws[5] = jnp.where(z_down, ws[5], 0.0)
                    for j, w in enumerate(ws):
                        r["W"][6 * (2 * b + a) + j] = inv * w
        start = [[got(2 * b + a) for a in (0, 1)] for b in (0, 1)]

        def coarse(_, flat):
            c = [[flat[0], flat[1]], [flat[2], flat[3]]]
            new = []
            for b in (0, 1):
                for a in (0, 1):
                    t = [r["W"][6 * (2 * b + a) + j] * n for j, n in enumerate(sides(c, b, a))]
                    v = start[b][a] + (1.0 - OMEGA) * c[b][a]
                    new.append((v + (t[0] + t[1])) + ((t[2] + t[3]) + (t[4] + t[5])))
            return tuple(new)

        flat = (start[0][0], start[0][1], start[1][0], start[1][1])
        flat = lax.fori_loop(0, SWEEPS - 1, coarse, flat)

        ring = r["VF2"].at[cyc]
        remote(ring.at[0:6], ring.at[0:6], S_SEM + cyc, 1, 0).wait_recv()
        cell = row // 2
        want = (lane & ~7) + (R - 1) + (cell + 1) // 2
        full2 = {}
        for i in range(8):
            v = ring[i]
            if 2 <= i < 6:
                v = jnp.where((row >= 2) & (row < 6), v2[i], v)
            full2[i] = jnp.where(r["K2"][i] > 0.0, v, 0.0)
        for i in range(4):
            s, a = R - 1 + (i + 1) // 2, (i + 1) % 2
            e0 = jnp.broadcast_to(flat[a][s : s + 1], (8, 128))
            e1 = jnp.broadcast_to(flat[2 + a][s : s + 1], (8, 128))
            e = jnp.take_along_axis(jnp.where(cell % 2 == 0, e1, e0), want, axis=1)
            r["VE2"][2 * i] = full2[2 * i] + e
            r["VE2"][2 * i + 1] = full2[2 * i + 1] + e

        up2 = {}
        for i in range(1, 7):
            v, n = around(2, r["VE2"], i)
            up2[i] = (1.0 - OMEGA) * v + full2[i] + r["I2"][i] * n
        for i in range(1, 7):
            r["S2"][i, pl.ds(0, 8, 2), :] = up2[i]
            r["S2"][i, pl.ds(1, 8, 2), :] = up2[i]

        unrolled(2, 14, lambda i: [(r["VE1"], i, r["V1"][i] + r["S2"][i // 2])])

        def up1(j, _):
            new = []
            for q in range(5):
                i = 3 + 5 * j + q
                v, n = around(1, r["VE1"], i)
                new.append((i, (1.0 - OMEGA) * v + r["V1"][i] + r["I1"][i] * n))
            for i, v in new:
                r["F1"][i, pl.ds(0, 16, 2), :] = v
                r["F1"][i, pl.ds(1, 16, 2), :] = v
            return 0

        lax.fori_loop(0, 2, up1, 0)

        def add0(i):
            e = r["F1"][i]
            return [(r["VE"], 2 * i + q, r["V"][2 * i + q] + e) for q in (0, 1)]

        planes(3, 13, 5, add0)

        def up0(i, c=cyc):
            v, n = around(0, r["VE"], i)
            if c == 0:
                v = (1.0 - OMEGA) * v + r["V"][i] + r["I0"][i] * n
            else:
                v = (1.0 - OMEGA) * v + r["I0"][i] * (r["G"][i] + n)
            v = v[8:24]
            if c == CYCLES - 1:
                return [(out, i - 8, v)]
            return [(r["VB"].at[:, 8:24], i, v), (r["F0"], i - 8, v)]

        planes(8, 24, 4, up0)
        if cyc < CYCLES - 1:
            send_field()

    for name in SEM:
        y_faces(name).wait_send()
        the_rest(name).wait_send()
    field(0).wait_send()
    field(1).wait_send()
    for cyc in range(CYCLES):
        ring = r["VF2"].at[cyc, 0:6]
        remote(ring, ring, S_SEM + cyc, 1, 0).wait_send()
        rows = r["C"].at[cyc, 0 : len(PARTNERS)]
        remote(rows, rows, C_SEM + cyc, 1, 0).wait_send()


SEM = {"M": 0, "G": 2}
V_SEM, S_SEM, C_SEM = 4, 6, 6 + CYCLES
CUT = {"M": 8, "G": 6, "VB": 7}
FILL = {"M": "FM", "G": "FZ"}
SPARE = {"M": "MS", "G": "GS"}
FOUR = ((1, 0), (-1, 0), (0, 1), (0, -1))


def scratch():
    f = jnp.float32

    def vm(*shape):
        return pltpu.VMEM(shape, f)

    a, b, c = vm(32, 32, 128), vm(16, 16, 128), vm(8, 8, 128)
    dma = pltpu.SemaphoreType.DMA
    shapes = [a, pltpu.VMEM((32, 32, 128), jnp.int32)] + [a] * 9
    shapes += [vm(16, 32, 128)] * 2 + [b] * 8 + [vm(8, 16, 128)] * 2
    shapes += [c] + [vm(CYCLES, 8, 8, 128)] * 2 + [c] * 5 + [vm(4, 8, 128), b]
    shapes += [vm(CYCLES, 64, 128), vm(24, 8, 128)]
    sems = C_SEM + CYCLES
    i16, i32 = (pltpu.VMEM((n, n, 128), jnp.int32) for n in (16, 32))
    shapes += [i16, b, i32, a, a]
    return shapes + [dma((2,)), dma((sems,)), dma((sems,)), pltpu.SemaphoreType.REGULAR((3,))]


def local(right_side, material, conductivity):
    nx, ny = lax.axis_size("gx"), lax.axis_size("gy")
    return pl.pallas_call(
        functools.partial(kernel, nx, ny),
        out_shape=pltpu.VMEM(right_side.shape, right_side.dtype),
        in_specs=[
            pl.BlockSpec(memory_space=pltpu.SMEM),
            pl.BlockSpec(memory_space=pl.ANY),
            pl.BlockSpec(memory_space=pl.ANY),
        ],
        out_specs=pl.BlockSpec(memory_space=pltpu.VMEM),
        scratch_shapes=scratch(),
        compiler_params=pltpu.CompilerParams(collective_id=0, has_side_effects=True),
        name="vcycles",
    )(conductivity, right_side, material)


def solution(mesh):
    return jax.shard_map(
        local,
        mesh=mesh,
        in_specs=(P("gx", "gy", None), P("gx", "gy", None), P()),
        out_specs=P("gx", "gy", None),
        check_vma=False,
    )
```
